32 devices in a mesh: grp: 2 (over y), seq: 4 (over z), head: 4 (over x, core).
Axes of the slice: x: 2, y: 2, z: 4, core: 2. Of those that a mesh axis runs over, the one named last changes fastest.
Arguments:
- token_queries: bfloat16 [4, 1024, 4096], P('grp', 'seq', 'head'), parts along dimension 0, may hold values from -6 to 6
- token_keys: bfloat16 [4, 1024, 4096], P('grp', 'seq', 'head'), parts along dimension 0, may hold values from -6 to 6
- token_values: bfloat16 [4, 1024, 4096], P('grp', 'seq', 'head'), parts along dimension 0, may hold values from -6 to 6
- step_size: float32 [8, 4, 1024], P('head', 'grp', 'seq'), parts along dimension 1, may hold values from 0.5 to 9
- fast_weights: float32 [6, 8, 512, 512], P('grp', 'head', 'seq'), parts along dimension 0, may hold values from -0.25 to 0.25
- momentum: float32 [6, 8, 512, 512], P('grp', 'head', 'seq'), parts along dimension 0, may hold values from -0.1875 to 0.1875
- fast_gain: float32 [8, 512], P('head'), may hold values from 0.5 to 1.5
Outputs:
- layer_out: bfloat16 [4, 1024, 4096], P('grp', 'seq', 'head'), parts along dimension 0
- new_weights: float32 [6, 8, 512, 512], P('grp', 'head', 'seq'), parts along dimension 0
- new_momentum: float32 [6, 8, 512, 512], P('grp', 'head', 'seq'), parts along dimension 0
The draws below stay inside these ranges and needn't reach their ends.
There are 2 independent parts, one for each index of `grp`. The reference program is written for one: setup_inputs(seed, part) draws one part's arguments, and reference() takes and returns one part's arrays. A program takes and returns all parts, laid end to end along the dimension named above; an argument that names none is the same for every part. Nothing has to cross between parts.
All inputs are finite; a program needn't handle non-finite values.
Results may differ from the reference program's by a relative error of at most 0.025.
Values may be sent and summed in bfloat16 or wider, within the bound.
A program may use at most 64 MiB of HBM per device.

```python
import math
import jax
import jax.numpy as jnp
from jax import lax

HD = 128
FH = 8
FD = 512
WINDOW = 256
CH_DEV = 256
GROUP = 1024
FEAT = 4096
N_SEQ = 4


def token_field(key, salt):
    noise_key, scale_key = jax.random.split(jax.random.fold_in(key, salt))
    noise = jax.random.normal(noise_key, (2 * GROUP, FH * FD), jnp.float32)
    scales = jnp.exp(jax.random.uniform(scale_key, (2 * GROUP, 1), jnp.float32, jnp.log(0.5), jnp.log(2.0)))
    return jnp.clip(noise * scales, -6.0, 6.0)


def draw_token_queries(key, part):
    field = token_field(key, 11)
    return field.reshape(2, GROUP, FH * FD).astype(jnp.bfloat16)


def draw_token_keys(key, part):
    field = token_field(key, 13)
    return field.reshape(2, GROUP, FH * FD).astype(jnp.bfloat16)


def draw_step_size(key, part):
    position = jnp.arange(GROUP, dtype=jnp.float32) / GROUP
    ramp = 1.0 + 2.0 * position
    jitter = jnp.exp(jax.random.uniform(jax.random.fold_in(key, 17), (FH, 2, GROUP), jnp.float32, jnp.log(0.5), 0.0))
    return (ramp[None, None, :] * jitter).astype(jnp.float32)


def raised(values, rng, source, target, parts, factor):
    def block_of(dim):
        return (jnp.arange(values.shape[dim]) // (values.shape[dim] // parts)).reshape((-1,) + (1,) * (values.ndim - 1 - dim))

    first = jax.random.permutation(rng, parts)[block_of(target)]
    other_side = (block_of(target) + parts // 2) % parts
    return jnp.where((block_of(source) == first) | (block_of(source) == other_side), factor * values, values)


def steps_of(rng, dims, cuts, smallest, largest):
    factor_of, own = 1.0, jax.random.fold_in(rng, 6)
    for dim, shards_of in cuts:
        steps = jnp.exp(jax.random.uniform(jax.random.fold_in(own, dim), (shards_of,), jnp.float32, smallest / len(cuts), largest / len(cuts)))
        factor_of = factor_of * jnp.repeat(steps, dims[dim] // shards_of).reshape([-1 if axis == dim else 1 for axis in range(len(dims))])
    return factor_of


def gaussian(own_key, dims, width, most, shards=(), held_as=jnp.bfloat16):
    drawn = jax.random.normal(own_key, dims, jnp.float32) * width
    if len(shards) > 0:
        drawn = steps_of(own_key, dims, shards, -0.22, 0.18) * drawn
    return jnp.clip(drawn, min=-most, max=most).astype(held_as)


def bell_draw_with(own_key, extent, width, limit, pieces, heavy, held_as=jnp.bfloat16):
    values = width * jax.random.normal(own_key, extent, jnp.float32)
    if pieces:
        values = values * steps_of(own_key, extent, pieces, -0.22, 0.18)
    return jnp.clip(raised(values, jax.random.fold_in(own_key, 3), *heavy), -limit, limit).astype(held_as)


def setup_inputs(seed: int = 0, part: int = 0) -> dict:
    arg_keys = jax.random.split(jax.random.key(seed), 8)
    part_splits = jax.random.split(jax.random.fold_in(arg_keys[7], part), 8)
    token_queries = draw_token_queries(jax.random.fold_in(jax.random.fold_in(arg_keys[7], part), 71), part)
    token_keys = draw_token_keys(jax.random.fold_in(jax.random.fold_in(arg_keys[7], part), 71), part)
    token_values = bell_draw_with(part_splits[2], (2, GROUP, FEAT), 1.0, 6.0, ((1, 4), (2, 4)), (1, 2, 4, 2.0))
    step_size = draw_step_size(jax.random.fold_in(jax.random.fold_in(arg_keys[7], part), 71), part)
    fast_weights = gaussian(part_splits[4], (3, FH, FD, FD), FD ** -0.5, 0.25, ((1, 4), (2, 4)), jnp.float32)
    momentum = gaussian(part_splits[5], (3, FH, FD, FD), (0.6 / GROUP ** 0.5), 0.1875, ((1, 4), (2, 4)), jnp.float32)
    fast_gain = jnp.clip(1.0 + 0.1 * jax.random.normal(arg_keys[6], (FH, FD), jnp.float32), 0.5, 1.5)
    return dict(token_queries=token_queries, token_keys=token_keys, token_values=token_values, step_size=step_size, fast_weights=fast_weights, momentum=momentum, fast_gain=fast_gain)


EPSILON = 1e-06
MOMENT_DECAY = 0.9
STEP_RATE = 0.02

def rms_rows(values):
    return values * lax.rsqrt(lax.optimization_barrier(jnp.mean(values * values, axis=-1, keepdims=True)) + EPSILON)

def attention(token_queries, token_keys, token_values):
    blocks = 2 * GROUP // CH_DEV
    head_count = FH * FD // HD
    query_blocks = token_queries.reshape(blocks, CH_DEV, head_count, HD)
    key_blocks = token_keys.reshape(blocks, CH_DEV, head_count, HD)
    value_blocks = token_values.reshape(blocks, CH_DEV, head_count, HD)
    key_prior = jnp.concatenate([jnp.zeros_like(key_blocks[:1]), key_blocks[:-1]], axis=0)[:, CH_DEV - WINDOW:]
    value_prior = jnp.concatenate([jnp.zeros_like(value_blocks[:1]), value_blocks[:-1]], axis=0)[:, CH_DEV - WINDOW:]
    query_pos = jnp.arange(CH_DEV, dtype=jnp.int32)[:, None]
    key_pos = jnp.arange(WINDOW + CH_DEV, dtype=jnp.int32)[None, :] - WINDOW
    band = (key_pos <= query_pos) & (key_pos > query_pos - WINDOW)
    score_scale = 1.0 / math.sqrt(HD)

    def one_block(inputs):
        query_block, key_block, value_block, key_back, value_back, index = inputs
        key_all = jnp.concatenate([key_back, key_block], 0).astype(jnp.float32)
        value_all = jnp.concatenate([value_back, value_block], 0).astype(jnp.float32)
        scores = jnp.einsum('qhd,khd->hqk', query_block.astype(jnp.float32), key_all) * score_scale
        allowed = band & ((key_pos >= 0) | (index > 0))
        scores = jnp.where(allowed[None], scores, -1e+30)
        top = lax.optimization_barrier(jnp.max(scores, axis=-1, keepdims=True))
        expo = jnp.exp(scores - top)
        probs = (expo / lax.optimization_barrier(jnp.sum(expo, axis=-1, keepdims=True))).astype(jnp.bfloat16)
        mixed = jnp.einsum('hqk,khd->qhd', probs.astype(jnp.float32), value_all)
        return mixed.reshape(CH_DEV, head_count * HD)
    result = lax.map(one_block, (query_blocks, key_blocks, value_blocks, key_prior, value_prior, jnp.arange(blocks, dtype=jnp.int32)))
    return result.reshape(2, GROUP, head_count * HD)

def shard_rows(values):
    return values.astype(jnp.float32).reshape(N_SEQ, CH_DEV, FD)

def fast_head(inputs):
    query_head, key_head, value_head, rates, weights, moment, gain = inputs
    results = []
    for period in range(2):
        casted = weights.astype(jnp.bfloat16)
        key_norm = rms_rows(key_head[period].astype(jnp.float32)).astype(jnp.bfloat16)
        gate_pre = jnp.dot(key_norm, casted[0].T, preferred_element_type=jnp.float32)
        up_pre = jnp.dot(key_norm, casted[1].T, preferred_element_type=jnp.float32)
        sigma = jax.nn.sigmoid(gate_pre)
        active = gate_pre * sigma
        slope = sigma * (1.0 + gate_pre * (1.0 - sigma))
        hidden = (active * up_pre).astype(jnp.bfloat16)
        targets = (rates[period][:, None] * value_head[period].astype(jnp.float32)).astype(jnp.bfloat16)
        back = -jnp.dot(targets, casted[2], preferred_element_type=jnp.float32)
        d_gate = (back * up_pre * slope).astype(jnp.bfloat16)
        d_up = (back * active).astype(jnp.bfloat16)
        g_gate = jnp.einsum('sti,stj->sij', shard_rows(d_gate), shard_rows(key_norm))
        g_up = jnp.einsum('sti,stj->sij', shard_rows(d_up), shard_rows(key_norm))
        g_down = -jnp.einsum('sto,sth->soh', shard_rows(targets), shard_rows(hidden))
        partial_value = jnp.stack([g_gate, g_up, g_down], axis=1)
        summed = lax.optimization_barrier(jnp.sum(lax.optimization_barrier(partial_value.astype(jnp.bfloat16)).astype(jnp.float32), axis=0))
        rate_total = jnp.sum(rates[period])
        moment = MOMENT_DECAY * moment + summed / rate_total
        weights = weights - STEP_RATE * rms_rows(moment)
        casted = weights.astype(jnp.bfloat16)
        query_norm = rms_rows(query_head[period].astype(jnp.float32)).astype(jnp.bfloat16)
        gate_q = jnp.dot(query_norm, casted[0].T, preferred_element_type=jnp.float32)
        up_q = jnp.dot(query_norm, casted[1].T, preferred_element_type=jnp.float32)
        hidden_q = (jax.nn.silu(gate_q) * up_q).astype(jnp.bfloat16)
        result = jnp.dot(hidden_q, casted[2].T, preferred_element_type=jnp.float32)
        results.append(rms_rows(result) * gain[None, :])
    return (jnp.stack(results), weights, moment)

def split_heads(values):
    return jnp.moveaxis(values.reshape(2, GROUP, FH, FD), 2, 0)

def reference(token_queries, token_keys, token_values, step_size, fast_weights, momentum, fast_gain):
    mixed = attention(token_queries, token_keys, token_values)
    fast_out, weights, moment = lax.map(fast_head, (split_heads(token_queries), split_heads(token_keys), split_heads(token_values), step_size, jnp.moveaxis(fast_weights, 1, 0), jnp.moveaxis(momentum, 1, 0), fast_gain))
    fast_out = jnp.moveaxis(fast_out, 0, 2).reshape(2, GROUP, FH * FD)
    layer_out = (mixed + fast_out).astype(jnp.bfloat16)
    return (layer_out, jnp.moveaxis(weights, 0, 1), jnp.moveaxis(moment, 0, 1))
```

```python
import math

import jax
import jax.numpy as jnp
from jax import lax
from jax.sharding import PartitionSpec as P

HD = 128
WINDOW = 256


EPSILON = 1e-06
MOMENT_DECAY = 0.9
STEP_RATE = 0.02


def shifted(block, axis, distance):
    devices = range(lax.axis_size(axis))
    route = [((i - distance) % len(devices), i) for i in devices]
    return lax.ppermute(block, axis, route)


def rms_rows(values):
    return values * lax.rsqrt(jnp.mean(values * values, axis=-1, keepdims=True) + EPSILON)


def attend(query_rows, key_rows, value_rows, halo_live, head_count):
    periods, row_count, features = query_rows.shape
    key_span = key_rows.shape[1]
    query_heads = query_rows.reshape(periods, row_count, head_count, HD)
    key_heads = key_rows.reshape(periods, key_span, head_count, HD)
    value_heads = value_rows.reshape(periods, key_span, head_count, HD)
    scores = jnp.einsum(
        "pqhd,pkhd->phqk", query_heads, key_heads, preferred_element_type=jnp.float32
    )
    scores = scores * (1.0 / math.sqrt(HD))
    query_pos = lax.broadcasted_iota(jnp.int32, (row_count, key_span), 0)
    key_pos = lax.broadcasted_iota(jnp.int32, (row_count, key_span), 1) - (key_span - row_count)
    band = (key_pos <= query_pos) & (key_pos > query_pos - WINDOW)
    allowed = band[None] & ((key_pos >= 0)[None] | halo_live[:, None, None])
    scores = jnp.where(allowed[:, None], scores, -1e30)
    top = jnp.max(scores, axis=-1, keepdims=True)
    expo = jnp.exp(scores - top)
    probs = (expo / jnp.sum(expo, axis=-1, keepdims=True)).astype(jnp.bfloat16)
    mixed = jnp.einsum("phqk,pkhd->pqhd", probs, value_heads, preferred_element_type=jnp.float32)
    return mixed.reshape(periods, row_count, features)


def silu_parts(pre):
    sigma = jax.nn.sigmoid(pre)
    return (pre * sigma, sigma * (1.0 + pre * (1.0 - sigma)))


def partial_grads(casted, key_norm, targets):
    gate_pre = jnp.einsum("thi,hji->htj", key_norm, casted[0], preferred_element_type=jnp.float32)
    up_pre = jnp.einsum("thi,hji->htj", key_norm, casted[1], preferred_element_type=jnp.float32)
    active, slope = silu_parts(gate_pre)
    hidden = (active * up_pre).astype(jnp.bfloat16)
    back = -jnp.einsum("tho,hoj->htj", targets, casted[2], preferred_element_type=jnp.float32)
    d_gate = (back * up_pre * slope).astype(jnp.bfloat16)
    d_up = (back * active).astype(jnp.bfloat16)
    g_gate = jnp.einsum("htj,thi->hji", d_gate, key_norm, preferred_element_type=jnp.float32)
    g_up = jnp.einsum("htj,thi->hji", d_up, key_norm, preferred_element_type=jnp.float32)
    g_down = -jnp.einsum("tho,htj->hoj", targets, hidden, preferred_element_type=jnp.float32)
    return jnp.stack([g_gate, g_up, g_down])


def apply_fast(casted, query_norm, fast_gain):
    gate_pre = jnp.einsum("thi,hji->htj", query_norm, casted[0], preferred_element_type=jnp.float32)
    up_pre = jnp.einsum("thi,hji->htj", query_norm, casted[1], preferred_element_type=jnp.float32)
    hidden = (jax.nn.silu(gate_pre) * up_pre).astype(jnp.bfloat16)
    result = jnp.einsum("htj,hoj->tho", hidden, casted[2], preferred_element_type=jnp.float32)
    return rms_rows(result) * fast_gain[None]


def advance(weights, moment, summed, rate_total):
    moment = MOMENT_DECAY * moment + summed / rate_total[None, :, None, None]
    weights = weights - STEP_RATE * rms_rows(moment)
    return (weights, moment)


def spread_rows(weights):
    return lax.all_gather(weights.astype(jnp.bfloat16), "seq", axis=2, tiled=True)


def split_shards(token_queries, token_keys, token_values, step_size, fast_weights, momentum, fast_gain):
    periods, row_count, features = token_queries.shape
    head_count = features // HD
    head_width = fast_weights.shape[3]
    fast_heads = features // head_width
    seq_place = lax.axis_index("seq")
    leading = seq_place == 0
    tail_rows = shifted((token_keys, token_values), "seq", 1)
    halo_keys = jnp.where(leading, jnp.roll(tail_rows[0], 1, axis=0), tail_rows[0])
    halo_values = jnp.where(leading, jnp.roll(tail_rows[1], 1, axis=0), tail_rows[1])
    halo_live = jnp.logical_or(jnp.logical_not(leading), jnp.arange(periods, dtype=jnp.int32) > 0)
    key_all = jnp.concatenate([halo_keys, token_keys], 1)
    value_all = jnp.concatenate([halo_values, token_values], 1)
    mixed_all = attend(token_queries, key_all, value_all, halo_live, head_count)
    weight_state, moment_state = (fast_weights, momentum)
    casted = spread_rows(weight_state)
    outputs = []
    for period in range(periods):
        rates = step_size[:, period]
        key_norm = rms_rows(
            token_keys[period].reshape(row_count, fast_heads, head_width).astype(jnp.float32)
        ).astype(jnp.bfloat16)
        targets = (
            rates.T[:, :, None]
            * token_values[period].reshape(row_count, fast_heads, head_width).astype(jnp.float32)
        ).astype(jnp.bfloat16)
        partial_value = partial_grads(casted, key_norm, targets)
        rate_total = lax.psum(jnp.sum(rates, axis=1), "seq")
        summed = lax.psum_scatter(
            partial_value.astype(jnp.bfloat16), "seq", scatter_dimension=2, tiled=True
        ).astype(jnp.float32)
        weight_state, moment_state = advance(weight_state, moment_state, summed, rate_total)
        casted = spread_rows(weight_state)
        query_norm = rms_rows(
            token_queries[period].reshape(row_count, fast_heads, head_width).astype(jnp.float32)
        ).astype(jnp.bfloat16)
        fast_out = apply_fast(casted, query_norm, fast_gain).reshape(row_count, features)
        outputs.append((mixed_all[period] + fast_out).astype(jnp.bfloat16))
    return (jnp.stack(outputs), weight_state, moment_state)


def collect(near, far):
    half = lax.axis_size("seq") // 2
    left = lax.axis_index("seq") < half
    nears = [near]
    for j in range(1, half):
        nears.append(lax.ppermute(near, "seq", [(half - 1 - j, half - 1), (half + j, half)]))
    fars = []
    for j in range(half):
        fars.append(lax.ppermute(far, "seq", [(half - 1 - j, half), (half + j, half - 1)]))
    slots = nears[::-1] + fars
    return [jnp.where(left, a, b) for a, b in zip(slots, slots[::-1])]


def deliver(blocks):
    half = lax.axis_size("seq") // 2
    me = lax.axis_index("seq")
    left = me < half
    slots = [jnp.where(left, a, b) for a, b in zip(blocks, blocks[::-1])]
    near, far = slots[half - 1], None
    place = jnp.where(left, half - 1 - me, me - half)
    for j in range(half):
        if j > 0:
            got = lax.ppermute(
                slots[half - 1 - j], "seq", [(half - 1, half - 1 - j), (half, half + j)]
            )
            near = jnp.where(place == j, got, near)
        got = lax.ppermute(slots[half + j], "seq", [(half, half - 1 - j), (half - 1, half + j)])
        far = got if far is None else jnp.where(place == j, got, far)
    return near, far


def grads_one(casted, key_norm, targets):
    gate_pre = jnp.einsum("ti,ji->tj", key_norm, casted[0], preferred_element_type=jnp.float32)
    up_pre = jnp.einsum("ti,ji->tj", key_norm, casted[1], preferred_element_type=jnp.float32)
    active, slope = silu_parts(gate_pre)
    hidden = (active * up_pre).astype(jnp.bfloat16)
    back = -jnp.einsum("to,oj->tj", targets, casted[2], preferred_element_type=jnp.float32)
    d_gate = (back * up_pre * slope).astype(jnp.bfloat16)
    d_up = (back * active).astype(jnp.bfloat16)
    g_gate = jnp.einsum("tj,ti->ji", d_gate, key_norm, preferred_element_type=jnp.float32)
    g_up = jnp.einsum("tj,ti->ji", d_up, key_norm, preferred_element_type=jnp.float32)
    g_down = -jnp.einsum("to,tj->oj", targets, hidden, preferred_element_type=jnp.float32)
    return [g_gate, g_up, g_down]


def apply_one(casted, query_norm, gain):
    gate_pre = jnp.einsum("ti,ji->tj", query_norm, casted[0], preferred_element_type=jnp.float32)
    up_pre = jnp.einsum("ti,ji->tj", query_norm, casted[1], preferred_element_type=jnp.float32)
    hidden = (jax.nn.silu(gate_pre) * up_pre).astype(jnp.bfloat16)
    result = jnp.einsum("tj,oj->to", hidden, casted[2], preferred_element_type=jnp.float32)
    return rms_rows(result) * gain[None]


def attend_blocks(query, keys, values, first):
    count, rows, width = query.shape
    heads = width // HD
    split = lambda x: x.reshape(count, rows, heads, HD)
    q = split(query)
    both = lambda x: jnp.concatenate([split(x[:-1]), split(x[1:])], 1)
    k, v = both(keys), both(values)
    scores = jnp.einsum("nqhd,nkhd->nhqk", q, k, preferred_element_type=jnp.float32)
    scores = scores * (1.0 / math.sqrt(HD))
    shape = (count, 1, rows, 2 * rows)
    block = lax.broadcasted_iota(jnp.int32, shape, 0)
    query_pos = lax.broadcasted_iota(jnp.int32, shape, 2)
    key_pos = lax.broadcasted_iota(jnp.int32, shape, 3) - rows
    allowed = (key_pos <= query_pos) & (key_pos > query_pos - WINDOW)
    if first:
        allowed = allowed & ((key_pos >= 0) | (block > 0))
    scores = jnp.where(allowed, scores, -1e30)
    top = jnp.max(scores, axis=-1, keepdims=True)
    expo = jnp.exp(scores - top)
    probs = (expo / jnp.sum(expo, axis=-1, keepdims=True)).astype(jnp.bfloat16)
    mixed = jnp.einsum("nhqk,nkhd->nqhd", probs, v, preferred_element_type=jnp.float32)
    return mixed.reshape(count, rows, width)


def hub_shards(
    token_queries, token_keys, token_values, step_size, fast_weights, momentum, fast_gain
):
    periods, rows, features = token_queries.shape
    width = fast_weights.shape[3]
    count = lax.axis_size("seq")
    left = lax.axis_index("seq") < count // 2

    def near_far(first, second):
        return jnp.where(left, first, second), jnp.where(left, second, first)

    def token_pair(array, period):
        return near_far(array[period, :, :width], array[period, :, width:])

    def row_pair(array):
        array = array.astype(jnp.bfloat16)
        return near_far(array[:, 0], array[:, 1])

    weight_blocks = collect(*row_pair(fast_weights))
    rate_blocks = collect(*near_far(step_size[0], step_size[1]))
    kv = [None] * periods
    queries = [None] * periods
    for period in range(periods):
        kn, kf = token_pair(token_keys, period)
        vn, vf = token_pair(token_values, period)
        kv[period] = collect(jnp.stack([kn, vn]), jnp.stack([kf, vf]))
        if period == 0:
            moment_blocks = collect(*row_pair(momentum))
        queries[period] = collect(*token_pair(token_queries, period))
    gain = jnp.where(left, fast_gain[0], fast_gain[1])
    weights = jnp.concatenate(weight_blocks, 1).astype(jnp.float32)
    moment = jnp.concatenate(moment_blocks, 1).astype(jnp.float32)
    hub_w = [weights[i] for i in range(3)]
    hub_m = [moment[i] for i in range(3)]
    casted = [w.astype(jnp.bfloat16) for w in hub_w]
    own_w, own_m = fast_weights, momentum
    prior = None
    outs = []
    for period in range(periods):
        keys = jnp.stack([b[0] for b in kv[period]])
        values = jnp.stack([b[1] for b in kv[period]])
        query = jnp.stack(queries[period])
        rates = jnp.concatenate([b[period] for b in rate_blocks])
        flat_k = keys.reshape(count * rows, width).astype(jnp.float32)
        flat_v = values.reshape(count * rows, width).astype(jnp.float32)
        flat_q = query.reshape(count * rows, width).astype(jnp.float32)
        key_norm = rms_rows(flat_k).astype(jnp.bfloat16)
        targets = (rates[:, None] * flat_v).astype(jnp.bfloat16)
        grads = grads_one(casted, key_norm, targets)
        total = jnp.sum(rates)
        steps = [g / total for g in grads]
        hub_m = [MOMENT_DECAY * m + s for m, s in zip(hub_m, steps)]
        hub_w = [w - STEP_RATE * rms_rows(m) for w, m in zip(hub_w, hub_m)]
        casted = [w.astype(jnp.bfloat16) for w in hub_w]
        sent = jnp.stack([s.astype(jnp.bfloat16) for s in steps])
        share = width // count
        near, far = deliver([sent[:, i * share : (i + 1) * share] for i in range(count)])
        mine = jnp.stack(near_far(near, far), 1).astype(jnp.float32)
        own_m = MOMENT_DECAY * own_m + mine
        own_w = own_w - STEP_RATE * rms_rows(own_m)
        query_norm = rms_rows(flat_q).astype(jnp.bfloat16)
        fast = apply_one(casted, query_norm, gain).reshape(count, rows, width)
        before = jnp.zeros_like(keys[:1]), jnp.zeros_like(values[:1])
        if prior is not None:
            before = prior
        mixed = attend_blocks(
            query,
            jnp.concatenate([before[0], keys]),
            jnp.concatenate([before[1], values]),
            period == 0,
        )
        prior = keys[-1:], values[-1:]
        layer = (mixed + fast).astype(jnp.bfloat16)
        near, far = deliver([layer[i] for i in range(count)])
        outs.append(jnp.concatenate(near_far(near, far), 1))
    return jnp.stack(outs), own_w, own_m


def shards(token_queries, token_keys, token_values, step_size, fast_weights, momentum, fast_gain):
    args = (
        token_queries,
        token_keys,
        token_values,
        step_size,
        fast_weights,
        momentum,
        fast_gain,
    )
    two_hubs = fast_weights.shape[1] == 2 and lax.axis_size("seq") % 2 == 0
    return hub_shards(*args) if two_hubs else split_shards(*args)


def solution(mesh):
    placed = (
        P("grp", "seq", "head"),
        P("grp", "seq", "head"),
        P("grp", "seq", "head"),
        P("head", "grp", "seq"),
        P("grp", "head", "seq", None),
        P("grp", "head", "seq", None),
        P("head", None),
    )
    return jax.shard_map(
        shards,
        mesh=mesh,
        in_specs=placed,
        out_specs=(
            P("grp", "seq", "head"),
            P("grp", "head", "seq", None),
            P("grp", "head", "seq", None),
        ),
        check_vma=False,
    )
```

```python
import functools
import math

import jax
import jax.numpy as jnp
from jax import lax
from jax.experimental import pallas as pl
from jax.experimental.pallas import tpu as pltpu
from jax.sharding import PartitionSpec as P

HD = 128
WINDOW = 256


EPSILON = 1e-06
MOMENT_DECAY = 0.9
STEP_RATE = 0.02


def shifted(block, axis, distance):
    devices = range(lax.axis_size(axis))
    route = [((i - distance) % len(devices), i) for i in devices]
    return lax.ppermute(block, axis, route)


def rms_rows(values):
    return values * lax.rsqrt(jnp.mean(values * values, axis=-1, keepdims=True) + EPSILON)


def attend(query_rows, key_rows, value_rows, halo_live, head_count):
    periods, row_count, features = query_rows.shape
    key_span = key_rows.shape[1]
    query_heads = query_rows.reshape(periods, row_count, head_count, HD)
    key_heads = key_rows.reshape(periods, key_span, head_count, HD)
    value_heads = value_rows.reshape(periods, key_span, head_count, HD)
    scores = jnp.einsum(
        "pqhd,pkhd->phqk", query_heads, key_heads, preferred_element_type=jnp.float32
    )
    scores = scores * (1.0 / math.sqrt(HD))
    query_pos = lax.broadcasted_iota(jnp.int32, (row_count, key_span), 0)
    key_pos = lax.broadcasted_iota(jnp.int32, (row_count, key_span), 1) - (key_span - row_count)
    band = (key_pos <= query_pos) & (key_pos > query_pos - WINDOW)
    allowed = band[None] & ((key_pos >= 0)[None] | halo_live[:, None, None])
    scores = jnp.where(allowed[:, None], scores, -1e30)
    top = jnp.max(scores, axis=-1, keepdims=True)
    expo = jnp.exp(scores - top)
    probs = (expo / jnp.sum(expo, axis=-1, keepdims=True)).astype(jnp.bfloat16)
    mixed = jnp.einsum("phqk,pkhd->pqhd", probs, value_heads, preferred_element_type=jnp.float32)
    return mixed.reshape(periods, row_count, features)


def silu_parts(pre):
    sigma = jax.nn.sigmoid(pre)
    return (pre * sigma, sigma * (1.0 + pre * (1.0 - sigma)))


def partial_grads(casted, key_norm, targets):
    gate_pre = jnp.einsum("thi,hji->htj", key_norm, casted[0], preferred_element_type=jnp.float32)
    up_pre = jnp.einsum("thi,hji->htj", key_norm, casted[1], preferred_element_type=jnp.float32)
    active, slope = silu_parts(gate_pre)
    hidden = (active * up_pre).astype(jnp.bfloat16)
    back = -jnp.einsum("tho,hoj->htj", targets, casted[2], preferred_element_type=jnp.float32)
    d_gate = (back * up_pre * slope).astype(jnp.bfloat16)
    d_up = (back * active).astype(jnp.bfloat16)
    g_gate = jnp.einsum("htj,thi->hji", d_gate, key_norm, preferred_element_type=jnp.float32)
    g_up = jnp.einsum("htj,thi->hji", d_up, key_norm, preferred_element_type=jnp.float32)
    g_down = -jnp.einsum("tho,htj->hoj", targets, hidden, preferred_element_type=jnp.float32)
    return jnp.stack([g_gate, g_up, g_down])


def apply_fast(casted, query_norm, fast_gain):
    gate_pre = jnp.einsum("thi,hji->htj", query_norm, casted[0], preferred_element_type=jnp.float32)
    up_pre = jnp.einsum("thi,hji->htj", query_norm, casted[1], preferred_element_type=jnp.float32)
    hidden = (jax.nn.silu(gate_pre) * up_pre).astype(jnp.bfloat16)
    result = jnp.einsum("htj,hoj->tho", hidden, casted[2], preferred_element_type=jnp.float32)
    return rms_rows(result) * fast_gain[None]


def advance(weights, moment, summed, rate_total):
    moment = MOMENT_DECAY * moment + summed / rate_total[None, :, None, None]
    weights = weights - STEP_RATE * rms_rows(moment)
    return (weights, moment)


def spread_rows(weights):
    return lax.all_gather(weights.astype(jnp.bfloat16), "seq", axis=2, tiled=True)


def split_shards(token_queries, token_keys, token_values, step_size, fast_weights, momentum, fast_gain):
    periods, row_count, features = token_queries.shape
    head_count = features // HD
    head_width = fast_weights.shape[3]
    fast_heads = features // head_width
    seq_place = lax.axis_index("seq")
    leading = seq_place == 0
    tail_rows = shifted((token_keys, token_values), "seq", 1)
    halo_keys = jnp.where(leading, jnp.roll(tail_rows[0], 1, axis=0), tail_rows[0])
    halo_values = jnp.where(leading, jnp.roll(tail_rows[1], 1, axis=0), tail_rows[1])
    halo_live = jnp.logical_or(jnp.logical_not(leading), jnp.arange(periods, dtype=jnp.int32) > 0)
    key_all = jnp.concatenate([halo_keys, token_keys], 1)
    value_all = jnp.concatenate([halo_values, token_values], 1)
    mixed_all = attend(token_queries, key_all, value_all, halo_live, head_count)
    weight_state, moment_state = (fast_weights, momentum)
    casted = spread_rows(weight_state)
    outputs = []
    for period in range(periods):
        rates = step_size[:, period]
        key_norm = rms_rows(
            token_keys[period].reshape(row_count, fast_heads, head_width).astype(jnp.float32)
        ).astype(jnp.bfloat16)
        targets = (
            rates.T[:, :, None]
            * token_values[period].reshape(row_count, fast_heads, head_width).astype(jnp.float32)
        ).astype(jnp.bfloat16)
        partial_value = partial_grads(casted, key_norm, targets)
        rate_total = lax.psum(jnp.sum(rates, axis=1), "seq")
        summed = lax.psum_scatter(
            partial_value.astype(jnp.bfloat16), "seq", scatter_dimension=2, tiled=True
        ).astype(jnp.float32)
        weight_state, moment_state = advance(weight_state, moment_state, summed, rate_total)
        casted = spread_rows(weight_state)
        query_norm = rms_rows(
            token_queries[period].reshape(row_count, fast_heads, head_width).astype(jnp.float32)
        ).astype(jnp.bfloat16)
        fast_out = apply_fast(casted, query_norm, fast_gain).reshape(row_count, features)
        outputs.append((mixed_all[period] + fast_out).astype(jnp.bfloat16))
    return (jnp.stack(outputs), weight_state, moment_state)


def dot_rows(x, y):
    return lax.dot_general(x, y, (((1,), (1,)), ((), ())), preferred_element_type=jnp.float32)


def dot_tokens(x, y):
    return lax.dot_general(x, y, (((0,), (0,)), ((), ())), preferred_element_type=jnp.float32)


def dot_plain(x, y):
    return lax.dot_general(x, y, (((1,), (0,)), ((), ())), preferred_element_type=jnp.float32)


def hub_kernel(
    n,
    periods,
    q_ref,
    k_ref,
    v_ref,
    r_ref,
    wb_ref,
    mb_ref,
    w_ref,
    m_ref,
    gain_ref,
    layer_ref,
    nw_ref,
    nm_ref,
    qb,
    kb,
    vb,
    rb,
    wblk,
    mblk,
    wf,
    mf,
    gacc,
    gs,
    gin,
    lbuf,
    fast,
    in_send,
    in_recv,
    g_send,
    g_recv,
    l_send,
    l_recv,
):
    half = n // 2
    me = lax.axis_index("seq")
    rows, width = kb.shape[1], kb.shape[2]
    share = width // n
    left = me < half
    near_h = jnp.where(left, 0, 1)
    far_h = 1 - near_h
    near_hub = half - 1 + near_h
    far_hub = half - 1 + far_h
    is_hub = me == near_hub
    mesh_id = pl.DeviceIdType.MESH

    barrier = pltpu.get_barrier_semaphore()
    for z in range(n):

        @pl.when(me != z)
        def _():
            pl.semaphore_signal(barrier, inc=1, device_id={"seq": z}, device_id_type=mesh_id)

    pl.semaphore_wait(barrier, n - 1)

    def columns(h):
        return pl.ds(pl.multiple_of(h * width, width), width)

    def own_rows(z):
        return pl.ds(pl.multiple_of(z * share, share), share)

    inward = [
        (lambda h: wb_ref.at[:, h], lambda z: wblk.at[:, own_rows(z)]),
        (lambda h: r_ref.at[h], lambda z: rb.at[z]),
    ]

    def tokens(ref, buf, p):
        return (lambda h: ref.at[p, :, columns(h)], lambda z: buf.at[p * n + z])

    kind = {"w": 0, "r": 1}
    for p in range(periods):
        kind["k", p] = len(inward)
        inward.append(tokens(k_ref, kb, p))
        kind["v", p] = len(inward)
        inward.append(tokens(v_ref, vb, p))
        if p == 0:
            kind["m"] = len(inward)
            inward.append((lambda h: mb_ref.at[:, h], lambda z: mblk.at[:, own_rows(z)]))
        kind["q", p] = len(inward)
        inward.append(tokens(q_ref, qb, p))

    def in_remote(i, h, hub, which, z):
        src, dst = inward[i]
        return pltpu.make_async_remote_copy(
            src_ref=src(h),
            dst_ref=dst(z),
            send_sem=in_send.at[i, which],
            recv_sem=in_recv.at[i, z],
            device_id={"seq": hub},
            device_id_type=mesh_id,
        )

    def in_local(i):
        src, dst = inward[i]
        return pltpu.make_async_copy(src(near_h), dst(me), in_recv.at[i, me])

    for i in range(len(inward)):
        in_remote(i, far_h, far_hub, 1, me).start()

        @pl.when(is_hub)
        def _():
            in_local(i).start()

        @pl.when(jnp.logical_not(is_hub))
        def _():
            in_remote(i, near_h, near_hub, 0, me).start()

    def await_in(i):
        for z in range(n):

            @pl.when(me == z)
            def _():
                in_local(i).wait()

            @pl.when(me != z)
            def _():
                in_remote(i, near_h, far_hub, 0, z).wait_recv()

    def out_remote(what, p, z, h):
        if what == "g":
            src, dst, ss, rs = gs.at[p, z], gin.at[p, h], g_send, g_recv
        else:
            src, dst = lbuf.at[p * n + z], layer_ref.at[p, :, columns(h)]
            ss, rs = l_send, l_recv
        return pltpu.make_async_remote_copy(
            src_ref=src,
            dst_ref=dst,
            send_sem=ss.at[p, z],
            recv_sem=rs.at[p, h],
            device_id={"seq": z},
            device_id_type=mesh_id,
        )

    def out_local(what, p):
        if what == "g":
            return pltpu.make_async_copy(gs.at[p, me], gin.at[p, near_h], g_recv.at[p, near_h])
        return pltpu.make_async_copy(
            lbuf.at[p * n + me], layer_ref.at[p, :, columns(near_h)], l_recv.at[p, near_h]
        )

    def send_out(what, p):
        for z in range(n):

            @pl.when(me == z)
            def _():
                out_local(what, p).start()

            @pl.when(me != z)
            def _():
                out_remote(what, p, z, near_h).start()

    def await_out(what, p):
        for h in range(2):

            @pl.when(me == half - 1 + h)
            def _():
                out_local(what, p).wait()

            @pl.when(me != half - 1 + h)
            def _():
                out_remote(what, p, half - 1 + h, h).wait_recv()

    def rate_total(p):
        total = jnp.sum(rb[0, p : p + 1, :], axis=1, keepdims=True)
        for z in range(1, n):
            total = total + jnp.sum(rb[z, p : p + 1, :], axis=1, keepdims=True)
        return total

    @pl.when(is_hub)
    def _():
        gain = gain_ref[pl.ds(near_h, 1), :]
        row_pos = lax.broadcasted_iota(jnp.int32, (rows, rows), 0)
        col_pos = lax.broadcasted_iota(jnp.int32, (rows, rows), 1)
        causal = col_pos <= row_pos
        await_in(kind["w"])
        await_in(kind["r"])
        for p in range(periods):
            await_in(kind["k", p])
            await_in(kind["v", p])
            gacc[...] = jnp.zeros_like(gacc)

            def grad_step(z, carry):
                key_norm = rms_rows(kb[p * n + z].astype(jnp.float32)).astype(jnp.bfloat16)
                gate_pre = dot_rows(key_norm, wblk[0])
                up_pre = dot_rows(key_norm, wblk[1])
                rates = jnp.broadcast_to(rb[z, p : p + 1, :], (HD, rows)).T[:, :1]
                targets = (rates * vb[p * n + z].astype(jnp.float32)).astype(jnp.bfloat16)
                back = -dot_plain(targets, wblk[2])
                active, slope = silu_parts(gate_pre)
                hidden = (active * up_pre).astype(jnp.bfloat16)
                d_gate = (back * up_pre * slope).astype(jnp.bfloat16)
                d_up = (back * active).astype(jnp.bfloat16)
                gacc[0] += dot_tokens(d_gate, key_norm)
                gacc[1] += dot_tokens(d_up, key_norm)
                gacc[2] -= dot_tokens(targets, hidden)
                return carry

            lax.fori_loop(0, n, grad_step, 0)
            if p == 0:
                await_in(kind["m"])
            total = rate_total(p)

            def update_step(z, carry):
                part = own_rows(z)
                for i in range(3):
                    step = gacc[i, part, :] / total
                    gs[p, z, i] = step.astype(jnp.bfloat16)
                    old_m = mblk[i, part, :].astype(jnp.float32) if p == 0 else mf[i, part, :]
                    old_w = wblk[i, part, :].astype(jnp.float32) if p == 0 else wf[i, part, :]
                    moment = MOMENT_DECAY * old_m + step
                    weight = old_w - STEP_RATE * rms_rows(moment)
                    mf[i, part, :] = moment
                    wf[i, part, :] = weight
                    wblk[i, part, :] = weight.astype(jnp.bfloat16)
                return carry

            lax.fori_loop(0, n, update_step, 0)
            await_in(kind["q", p])
            send_out("g", p)

            def apply_step(z, carry):
                g = p * n + z
                query_norm = rms_rows(qb[g].astype(jnp.float32)).astype(jnp.bfloat16)
                gate_pre = dot_rows(query_norm, wblk[0])
                up_pre = dot_rows(query_norm, wblk[1])
                hidden = (jax.nn.silu(gate_pre) * up_pre).astype(jnp.bfloat16)
                fast[...] = rms_rows(dot_rows(hidden, wblk[2])) * gain
                before = jnp.maximum(g - 1, 0)
                for head in range(width // HD):
                    cut = slice(head * HD, (head + 1) * HD)
                    query = qb[g, :, cut]
                    here = dot_rows(query, kb[g, :, cut])
                    past = dot_rows(query, kb[before, :, cut])
                    past = jnp.where(g > 0, past, -1e30 * math.sqrt(HD))
                    scores = jnp.where(causal, here, past) * (1.0 / math.sqrt(HD))
                    top = jnp.max(scores, axis=-1, keepdims=True)
                    expo = jnp.exp(scores - top)
                    probs = expo / jnp.sum(expo, axis=-1, keepdims=True)
                    own = jnp.where(causal, probs, 0.0).astype(jnp.bfloat16)
                    old = jnp.where(causal, 0.0, probs).astype(jnp.bfloat16)
                    mixed = dot_plain(own, vb[g, :, cut]) + dot_plain(old, vb[before, :, cut])
                    lbuf[g, :, cut] = (mixed + fast[:, cut]).astype(jnp.bfloat16)
                return carry

            lax.fori_loop(0, n, apply_step, 0)
            send_out("l", p)

    def own_step(h):
        for i in range(3):
            moment = m_ref[i, h]
            weight = w_ref[i, h]
            for p in range(periods):
                moment = MOMENT_DECAY * moment + gin[p, h, i].astype(jnp.float32)
                weight = weight - STEP_RATE * rms_rows(moment)
            nm_ref[i, h] = moment
            nw_ref[i, h] = weight

    for p in range(periods):
        await_out("g", p)
    for h in range(2):
        own_step(h)
    for p in range(periods):
        await_out("l", p)

    @pl.when(is_hub)
    def _():
        for p in range(periods):
            for z in range(n):

                @pl.when(me != z)
                def _():
                    out_remote("g", p, z, near_h).wait_send()
                    out_remote("l", p, z, near_h).wait_send()

    for i in range(len(inward)):
        in_remote(i, far_h, far_hub, 1, me).wait_send()

        @pl.when(jnp.logical_not(is_hub))
        def _():
            in_remote(i, near_h, near_hub, 0, me).wait_send()


def hub_shards(
    token_queries, token_keys, token_values, step_size, fast_weights, momentum, fast_gain
):
    periods, rows, features = token_queries.shape
    parts, heads, share, width = fast_weights.shape
    n = lax.axis_size("seq")
    bf16, f32 = jnp.bfloat16, jnp.float32
    kinds = 3 + 3 * periods
    vmem = pl.BlockSpec(memory_space=pltpu.VMEM)
    anywhere = pl.BlockSpec(memory_space=pl.ANY)
    square = (parts, width, width)
    stream = pltpu.VMEM((periods * n, rows, width), bf16)
    dma = pltpu.SemaphoreType.DMA
    return pl.pallas_call(
        functools.partial(hub_kernel, n, periods),
        out_shape=(
            jax.ShapeDtypeStruct(token_queries.shape, bf16),
            jax.ShapeDtypeStruct(fast_weights.shape, f32),
            jax.ShapeDtypeStruct(momentum.shape, f32),
        ),
        in_specs=[anywhere] * 6 + [vmem] * 3,
        out_specs=(anywhere, vmem, vmem),
        scratch_shapes=[
            stream,
            stream,
            stream,
            pltpu.VMEM((n, periods, rows), f32),
            pltpu.VMEM(square, bf16),
            pltpu.VMEM(square, bf16),
            pltpu.VMEM(square, f32),
            pltpu.VMEM(square, f32),
            pltpu.VMEM(square, f32),
            pltpu.VMEM((periods, n, parts, share, width), bf16),
            pltpu.VMEM((periods, heads, parts, share, width), bf16),
            stream,
            pltpu.VMEM((rows, width), f32),
            dma((kinds, 2)),
            dma((kinds, n)),
            dma((periods, n)),
            dma((periods, heads)),
            dma((periods, n)),
            dma((periods, heads)),
        ],
        compiler_params=pltpu.CompilerParams(
            collective_id=0, has_side_effects=True, vmem_limit_bytes=56 * 1024 * 1024
        ),
    )(
        token_queries,
        token_keys,
        token_values,
        step_size,
        fast_weights.astype(bf16),
        momentum.astype(bf16),
        fast_weights,
        momentum,
        fast_gain,
    )


def shards(token_queries, token_keys, token_values, step_size, fast_weights, momentum, fast_gain):
    args = (
        token_queries,
        token_keys,
        token_values,
        step_size,
        fast_weights,
        momentum,
        fast_gain,
    )
    n = lax.axis_size("seq")
    two_hubs = fast_weights.shape[1] == 2 and n % 2 == 0 and token_queries.shape[1] == WINDOW
    return hub_shards(*args) if two_hubs else split_shards(*args)


def solution(mesh):
    placed = (
        P("grp", "seq", "head"),
        P("grp", "seq", "head"),
        P("grp", "seq", "head"),
        P("head", "grp", "seq"),
        P("grp", "head", "seq", None),
        P("grp", "head", "seq", None),
        P("head", None),
    )
    return jax.shard_map(
        shards,
        mesh=mesh,
        in_specs=placed,
        out_specs=(
            P("grp", "seq", "head"),
            P("grp", "head", "seq", None),
            P("grp", "head", "seq", None),
        ),
        check_vma=False,
    )
```

```python
import functools
import math

import jax
import jax.numpy as jnp
from jax import lax
from jax.experimental import pallas as pl
from jax.experimental.pallas import tpu as pltpu
from jax.sharding import PartitionSpec as P

HD = 128
WINDOW = 256


EPSILON = 1e-06
MOMENT_DECAY = 0.9
STEP_RATE = 0.02


def shifted(block, axis, distance):
    devices = range(lax.axis_size(axis))
    route = [((i - distance) % len(devices), i) for i in devices]
    return lax.ppermute(block, axis, route)


def rms_rows(values):
    return values * lax.rsqrt(jnp.mean(values * values, axis=-1, keepdims=True) + EPSILON)


def attend(query_rows, key_rows, value_rows, halo_live, head_count):
    periods, row_count, features = query_rows.shape
    key_span = key_rows.shape[1]
    query_heads = query_rows.reshape(periods, row_count, head_count, HD)
    key_heads = key_rows.reshape(periods, key_span, head_count, HD)
    value_heads = value_rows.reshape(periods, key_span, head_count, HD)
    scores = jnp.einsum(
        "pqhd,pkhd->phqk", query_heads, key_heads, preferred_element_type=jnp.float32
    )
    scores = scores * (1.0 / math.sqrt(HD))
    query_pos = lax.broadcasted_iota(jnp.int32, (row_count, key_span), 0)
    key_pos = lax.broadcasted_iota(jnp.int32, (row_count, key_span), 1) - (key_span - row_count)
    band = (key_pos <= query_pos) & (key_pos > query_pos - WINDOW)
    allowed = band[None] & ((key_pos >= 0)[None] | halo_live[:, None, None])
    scores = jnp.where(allowed[:, None], scores, -1e30)
    top = jnp.max(scores, axis=-1, keepdims=True)
    expo = jnp.exp(scores - top)
    probs = (expo / jnp.sum(expo, axis=-1, keepdims=True)).astype(jnp.bfloat16)
    mixed = jnp.einsum("phqk,pkhd->pqhd", probs, value_heads, preferred_element_type=jnp.float32)
    return mixed.reshape(periods, row_count, features)


def silu_parts(pre):
    sigma = jax.nn.sigmoid(pre)
    return (pre * sigma, sigma * (1.0 + pre * (1.0 - sigma)))


def partial_grads(casted, key_norm, targets):
    gate_pre = jnp.einsum("thi,hji->htj", key_norm, casted[0], preferred_element_type=jnp.float32)
    up_pre = jnp.einsum("thi,hji->htj", key_norm, casted[1], preferred_element_type=jnp.float32)
    active, slope = silu_parts(gate_pre)
    hidden = (active * up_pre).astype(jnp.bfloat16)
    back = -jnp.einsum("tho,hoj->htj", targets, casted[2], preferred_element_type=jnp.float32)
    d_gate = (back * up_pre * slope).astype(jnp.bfloat16)
    d_up = (back * active).astype(jnp.bfloat16)
    g_gate = jnp.einsum("htj,thi->hji", d_gate, key_norm, preferred_element_type=jnp.float32)
    g_up = jnp.einsum("htj,thi->hji", d_up, key_norm, preferred_element_type=jnp.float32)
    g_down = -jnp.einsum("tho,htj->hoj", targets, hidden, preferred_element_type=jnp.float32)
    return jnp.stack([g_gate, g_up, g_down])


def apply_fast(casted, query_norm, fast_gain):
    gate_pre = jnp.einsum("thi,hji->htj", query_norm, casted[0], preferred_element_type=jnp.float32)
    up_pre = jnp.einsum("thi,hji->htj", query_norm, casted[1], preferred_element_type=jnp.float32)
    hidden = (jax.nn.silu(gate_pre) * up_pre).astype(jnp.bfloat16)
    result = jnp.einsum("htj,hoj->tho", hidden, casted[2], preferred_element_type=jnp.float32)
    return rms_rows(result) * fast_gain[None]


def advance(weights, moment, summed, rate_total):
    moment = MOMENT_DECAY * moment + summed / rate_total[None, :, None, None]
    weights = weights - STEP_RATE * rms_rows(moment)
    return (weights, moment)


def spread_rows(weights):
    return lax.all_gather(weights.astype(jnp.bfloat16), "seq", axis=2, tiled=True)


def split_shards(token_queries, token_keys, token_values, step_size, fast_weights, momentum, fast_gain):
    periods, row_count, features = token_queries.shape
    head_count = features // HD
    head_width = fast_weights.shape[3]
    fast_heads = features // head_width
    seq_place = lax.axis_index("seq")
    leading = seq_place == 0
    tail_rows = shifted((token_keys, token_values), "seq", 1)
    halo_keys = jnp.where(leading, jnp.roll(tail_rows[0], 1, axis=0), tail_rows[0])
    halo_values = jnp.where(leading, jnp.roll(tail_rows[1], 1, axis=0), tail_rows[1])
    halo_live = jnp.logical_or(jnp.logical_not(leading), jnp.arange(periods, dtype=jnp.int32) > 0)
    key_all = jnp.concatenate([halo_keys, token_keys], 1)
    value_all = jnp.concatenate([halo_values, token_values], 1)
    mixed_all = attend(token_queries, key_all, value_all, halo_live, head_count)
    weight_state, moment_state = (fast_weights, momentum)
    casted = spread_rows(weight_state)
    outputs = []
    for period in range(periods):
        rates = step_size[:, period]
        key_norm = rms_rows(
            token_keys[period].reshape(row_count, fast_heads, head_width).astype(jnp.float32)
        ).astype(jnp.bfloat16)
        targets = (
            rates.T[:, :, None]
            * token_values[period].reshape(row_count, fast_heads, head_width).astype(jnp.float32)
        ).astype(jnp.bfloat16)
        partial_value = partial_grads(casted, key_norm, targets)
        rate_total = lax.psum(jnp.sum(rates, axis=1), "seq")
        summed = lax.psum_scatter(
            partial_value.astype(jnp.bfloat16), "seq", scatter_dimension=2, tiled=True
        ).astype(jnp.float32)
        weight_state, moment_state = advance(weight_state, moment_state, summed, rate_total)
        casted = spread_rows(weight_state)
        query_norm = rms_rows(
            token_queries[period].reshape(row_count, fast_heads, head_width).astype(jnp.float32)
        ).astype(jnp.bfloat16)
        fast_out = apply_fast(casted, query_norm, fast_gain).reshape(row_count, features)
        outputs.append((mixed_all[period] + fast_out).astype(jnp.bfloat16))
    return (jnp.stack(outputs), weight_state, moment_state)


def dot_rows(x, y):
    return lax.dot_general(x, y, (((1,), (1,)), ((), ())), preferred_element_type=jnp.float32)


def dot_tokens(x, y):
    return lax.dot_general(x, y, (((0,), (0,)), ((), ())), preferred_element_type=jnp.float32)


def dot_plain(x, y):
    return lax.dot_general(x, y, (((1,), (0,)), ((), ())), preferred_element_type=jnp.float32)


def hub_kernel(
    n,
    periods,
    q_ref,
    k_ref,
    v_ref,
    r_ref,
    w_ref,
    m_ref,
    gain_ref,
    layer_ref,
    nw_ref,
    nm_ref,
    wb_ref,
    mb_ref,
    qb,
    kb,
    vb,
    rb,
    wblk,
    mblk,
    wf,
    mf,
    gacc,
    gs,
    gin,
    lbuf,
    fast,
    in_send,
    in_recv,
    g_send,
    g_recv,
    l_send,
    l_recv,
):
    half = n // 2
    me = lax.axis_index("seq")
    rows, width = kb.shape[1], kb.shape[2]
    share = width // n
    left = me < half
    near_h = jnp.where(left, 0, 1)
    far_h = 1 - near_h
    near_hub = half - 1 + near_h
    far_hub = half - 1 + far_h
    is_hub = me == near_hub
    mesh_id = pl.DeviceIdType.MESH

    barrier = pltpu.get_barrier_semaphore()
    for z in range(n):

        @pl.when(me != z)
        def _():
            pl.semaphore_signal(barrier, inc=1, device_id={"seq": z}, device_id_type=mesh_id)

    pl.semaphore_wait(barrier, n - 1)

    def columns(h):
        return pl.ds(pl.multiple_of(h * width, width), width)

    def own_rows(z):
        return pl.ds(pl.multiple_of(z * share, share), share)

    inward = []

    def tokens(ref, buf, p):
        return (lambda h: ref.at[p, :, columns(h)], lambda z: buf.at[p * n + z])

    kind = {}
    for p in range(periods):
        kind["k", p] = len(inward)
        inward.append(tokens(k_ref, kb, p))
        kind["v", p] = len(inward)
        inward.append(tokens(v_ref, vb, p))
        if p == 0:
            kind["w"] = len(inward)
            inward.append((lambda h: wb_ref.at[:, h], lambda z: wblk.at[:, own_rows(z)]))
            kind["r"] = len(inward)
            inward.append((lambda h: r_ref.at[h], lambda z: rb.at[z]))
            kind["m"] = len(inward)
            inward.append((lambda h: mb_ref.at[:, h], lambda z: mblk.at[:, own_rows(z)]))
        kind["q", p] = len(inward)
        inward.append(tokens(q_ref, qb, p))

    def in_remote(i, h, hub, which, z):
        src, dst = inward[i]
        return pltpu.make_async_remote_copy(
            src_ref=src(h),
            dst_ref=dst(z),
            send_sem=in_send.at[i, which],
            recv_sem=in_recv.at[i, z],
            device_id={"seq": hub},
            device_id_type=mesh_id,
        )

    def in_local(i):
        src, dst = inward[i]
        return pltpu.make_async_copy(src(near_h), dst(me), in_recv.at[i, me])

    for i in range(len(inward)):
        if i == kind["w"]:
            wb_ref[...] = w_ref[...].astype(jnp.bfloat16)
            mb_ref[...] = m_ref[...].astype(jnp.bfloat16)
        in_remote(i, far_h, far_hub, 1, me).start()

        @pl.when(is_hub)
        def _():
            in_local(i).start()

        @pl.when(jnp.logical_not(is_hub))
        def _():
            in_remote(i, near_h, near_hub, 0, me).start()

    def await_in(i):
        for z in range(n):

            @pl.when(me == z)
            def _():
                in_local(i).wait()

            @pl.when(me != z)
            def _():
                in_remote(i, near_h, far_hub, 0, z).wait_recv()

    def out_remote(what, p, z, h):
        if what == "g":
            src, dst, ss, rs = gs.at[p, z], gin.at[p, h], g_send, g_recv
        else:
            src, dst = lbuf.at[p * n + z], layer_ref.at[p, :, columns(h)]
            ss, rs = l_send, l_recv
        return pltpu.make_async_remote_copy(
            src_ref=src,
            dst_ref=dst,
            send_sem=ss.at[p, z],
            recv_sem=rs.at[p, h],
            device_id={"seq": z},
            device_id_type=mesh_id,
        )

    def out_local(what, p):
        if what == "g":
            return pltpu.make_async_copy(gs.at[p, me], gin.at[p, near_h], g_recv.at[p, near_h])
        return pltpu.make_async_copy(
            lbuf.at[p * n + me], layer_ref.at[p, :, columns(near_h)], l_recv.at[p, near_h]
        )

    def send_out(what, p):
        for z in range(n):

            @pl.when(me == z)
            def _():
                out_local(what, p).start()

            @pl.when(me != z)
            def _():
                out_remote(what, p, z, near_h).start()

    def await_out(what, p):
        for h in range(2):

            @pl.when(me == half - 1 + h)
            def _():
                out_local(what, p).wait()

            @pl.when(me != half - 1 + h)
            def _():
                out_remote(what, p, half - 1 + h, h).wait_recv()

    def rate_total(p):
        total = jnp.sum(rb[0, p : p + 1, :], axis=1, keepdims=True)
        for z in range(1, n):
            total = total + jnp.sum(rb[z, p : p + 1, :], axis=1, keepdims=True)
        return total

    @pl.when(is_hub)
    def _():
        gain = gain_ref[pl.ds(near_h, 1), :]
        row_pos = lax.broadcasted_iota(jnp.int32, (rows, rows), 0)
        col_pos = lax.broadcasted_iota(jnp.int32, (rows, rows), 1)
        causal = col_pos <= row_pos
        await_in(kind["w"])
        await_in(kind["r"])
        for p in range(periods):
            await_in(kind["k", p])
            await_in(kind["v", p])
            if p > 0:
                send_out("g", p - 1)
                send_out("l", p - 1)
            gacc[...] = jnp.zeros_like(gacc)

            def grad_step(z, carry):
                key_norm = rms_rows(kb[p * n + z].astype(jnp.float32)).astype(jnp.bfloat16)
                gate_pre = dot_rows(key_norm, wblk[0])
                up_pre = dot_rows(key_norm, wblk[1])
                rates = jnp.broadcast_to(rb[z, p : p + 1, :], (HD, rows)).T[:, :1]
                targets = (rates * vb[p * n + z].astype(jnp.float32)).astype(jnp.bfloat16)
                back = -dot_plain(targets, wblk[2])
                active, slope = silu_parts(gate_pre)
                hidden = (active * up_pre).astype(jnp.bfloat16)
                d_gate = (back * up_pre * slope).astype(jnp.bfloat16)
                d_up = (back * active).astype(jnp.bfloat16)
                gacc[0] += dot_tokens(d_gate, key_norm)
                gacc[1] += dot_tokens(d_up, key_norm)
                gacc[2] -= dot_tokens(targets, hidden)
                return carry

            lax.fori_loop(0, n, grad_step, 0)
            if p == 0:
                await_in(kind["m"])
            total = rate_total(p)

            def update_step(z, carry):
                part = own_rows(z)
                for i in range(3):
                    step = gacc[i, part, :] / total
                    gs[p, z, i] = step.astype(jnp.bfloat16)
                    old_m = mblk[i, part, :].astype(jnp.float32) if p == 0 else mf[i, part, :]
                    old_w = wblk[i, part, :].astype(jnp.float32) if p == 0 else wf[i, part, :]
                    moment = MOMENT_DECAY * old_m + step
                    weight = old_w - STEP_RATE * rms_rows(moment)
                    mf[i, part, :] = moment
                    wf[i, part, :] = weight
                    wblk[i, part, :] = weight.astype(jnp.bfloat16)
                return carry

            lax.fori_loop(0, n, update_step, 0)
            if p == periods - 1:
                send_out("g", p)
            await_in(kind["q", p])

            def apply_step(z, carry):
                g = p * n + z
                query_norm = rms_rows(qb[g].astype(jnp.float32)).astype(jnp.bfloat16)
                gate_pre = dot_rows(query_norm, wblk[0])
                up_pre = dot_rows(query_norm, wblk[1])
                hidden = (jax.nn.silu(gate_pre) * up_pre).astype(jnp.bfloat16)
                fast[...] = rms_rows(dot_rows(hidden, wblk[2])) * gain
                before = jnp.maximum(g - 1, 0)
                for head in range(width // HD):
                    cut = slice(head * HD, (head + 1) * HD)
                    query = qb[g, :, cut]
                    here = dot_rows(query, kb[g, :, cut])
                    past = dot_rows(query, kb[before, :, cut])
                    past = jnp.where(g > 0, past, -1e30 * math.sqrt(HD))
                    scores = jnp.where(causal, here, past) * (1.0 / math.sqrt(HD))
                    top = jnp.max(scores, axis=-1, keepdims=True)
                    expo = jnp.exp(scores - top)
                    probs = expo / jnp.sum(expo, axis=-1, keepdims=True)
                    own = jnp.where(causal, probs, 0.0).astype(jnp.bfloat16)
                    old = jnp.where(causal, 0.0, probs).astype(jnp.bfloat16)
                    mixed = dot_plain(own, vb[g, :, cut]) + dot_plain(old, vb[before, :, cut])
                    lbuf[g, :, cut] = (mixed + fast[:, cut]).astype(jnp.bfloat16)
                return carry

            lax.fori_loop(0, n, apply_step, 0)
            if p == periods - 1:
                send_out("l", p)

    def own_step(h):
        for i in range(3):
            moment = m_ref[i, h]
            weight = w_ref[i, h]
            for p in range(periods):
                moment = MOMENT_DECAY * moment + gin[p, h, i].astype(jnp.float32)
                weight = weight - STEP_RATE * rms_rows(moment)
            nm_ref[i, h] = moment
            nw_ref[i, h] = weight

    for p in range(periods):
        await_out("g", p)
    for h in range(2):
        own_step(h)
    for p in range(periods):
        await_out("l", p)

    @pl.when(is_hub)
    def _():
        for p in range(periods):
            for z in range(n):

                @pl.when(me != z)
                def _():
                    out_remote("g", p, z, near_h).wait_send()
                    out_remote("l", p, z, near_h).wait_send()

    for i in range(len(inward)):
        in_remote(i, far_h, far_hub, 1, me).wait_send()

        @pl.when(jnp.logical_not(is_hub))
        def _():
            in_remote(i, near_h, near_hub, 0, me).wait_send()


def hub_shards(
    token_queries, token_keys, token_values, step_size, fast_weights, momentum, fast_gain
):
    periods, rows, features = token_queries.shape
    parts, heads, share, width = fast_weights.shape
    n = lax.axis_size("seq")
    bf16, f32 = jnp.bfloat16, jnp.float32
    kinds = 3 + 3 * periods
    vmem = pl.BlockSpec(memory_space=pltpu.VMEM)
    anywhere = pl.BlockSpec(memory_space=pl.ANY)
    square = (parts, width, width)
    stream = pltpu.VMEM((periods * n, rows, width), bf16)
    dma = pltpu.SemaphoreType.DMA
    return pl.pallas_call(
        functools.partial(hub_kernel, n, periods),
        out_shape=(
            jax.ShapeDtypeStruct(token_queries.shape, bf16),
            jax.ShapeDtypeStruct(fast_weights.shape, f32),
            jax.ShapeDtypeStruct(momentum.shape, f32),
        ),
        in_specs=[anywhere] * 4 + [vmem] * 3,
        out_specs=(vmem, vmem, vmem),
        scratch_shapes=[
            pltpu.VMEM(fast_weights.shape, bf16),
            pltpu.VMEM(momentum.shape, bf16),
            stream,
            stream,
            stream,
            pltpu.VMEM((n, periods, rows), f32),
            pltpu.VMEM(square, bf16),
            pltpu.VMEM(square, bf16),
            pltpu.VMEM(square, f32),
            pltpu.VMEM(square, f32),
            pltpu.VMEM(square, f32),
            pltpu.VMEM((periods, n, parts, share, width), bf16),
            pltpu.VMEM((periods, heads, parts, share, width), bf16),
            stream,
            pltpu.VMEM((rows, width), f32),
            dma((kinds, 2)),
            dma((kinds, n)),
            dma((periods, n)),
            dma((periods, heads)),
            dma((periods, n)),
            dma((periods, heads)),
        ],
        compiler_params=pltpu.CompilerParams(
            collective_id=0, has_side_effects=True, vmem_limit_bytes=56 * 1024 * 1024
        ),
    )(
        token_queries,
        token_keys,
        token_values,
        step_size,
        fast_weights,
        momentum,
        fast_gain,
    )


def shards(token_queries, token_keys, token_values, step_size, fast_weights, momentum, fast_gain):
    args = (
        token_queries,
        token_keys,
        token_values,
        step_size,
        fast_weights,
        momentum,
        fast_gain,
    )
    n = lax.axis_size("seq")
    two_hubs = fast_weights.shape[1] == 2 and n % 2 == 0 and token_queries.shape[1] == WINDOW
    return hub_shards(*args) if two_hubs else split_shards(*args)


def solution(mesh):
    placed = (
        P("grp", "seq", "head"),
        P("grp", "seq", "head"),
        P("grp", "seq", "head"),
        P("head", "grp", "seq"),
        P("grp", "head", "seq", None),
        P("grp", "head", "seq", None),
        P("head", None),
    )
    return jax.shard_map(
        shards,
        mesh=mesh,
        in_specs=placed,
        out_specs=(
            P("grp", "seq", "head"),
            P("grp", "head", "seq", None),
            P("grp", "head", "seq", None),
        ),
        check_vma=False,
    )
```

```python
import functools
import math

import jax
import jax.numpy as jnp
from jax import lax
from jax.experimental import pallas as pl
from jax.experimental.pallas import tpu as pltpu
from jax.sharding import PartitionSpec as P

HD = 128
WINDOW = 256


EPSILON = 1e-06
MOMENT_DECAY = 0.9
STEP_RATE = 0.02


def shifted(block, axis, distance):
    devices = range(lax.axis_size(axis))
    route = [((i - distance) % len(devices), i) for i in devices]
    return lax.ppermute(block, axis, route)


def rms_rows(values):
    return values * lax.rsqrt(jnp.mean(values * values, axis=-1, keepdims=True) + EPSILON)


def attend(query_rows, key_rows, value_rows, halo_live, head_count):
    periods, row_count, features = query_rows.shape
    key_span = key_rows.shape[1]
    query_heads = query_rows.reshape(periods, row_count, head_count, HD)
    key_heads = key_rows.reshape(periods, key_span, head_count, HD)
    value_heads = value_rows.reshape(periods, key_span, head_count, HD)
    scores = jnp.einsum(
        "pqhd,pkhd->phqk", query_heads, key_heads, preferred_element_type=jnp.float32
    )
    scores = scores * (1.0 / math.sqrt(HD))
    query_pos = lax.broadcasted_iota(jnp.int32, (row_count, key_span), 0)
    key_pos = lax.broadcasted_iota(jnp.int32, (row_count, key_span), 1) - (key_span - row_count)
    band = (key_pos <= query_pos) & (key_pos > query_pos - WINDOW)
    allowed = band[None] & ((key_pos >= 0)[None] | halo_live[:, None, None])
    scores = jnp.where(allowed[:, None], scores, -1e30)
    top = jnp.max(scores, axis=-1, keepdims=True)
    expo = jnp.exp(scores - top)
    probs = (expo / jnp.sum(expo, axis=-1, keepdims=True)).astype(jnp.bfloat16)
    mixed = jnp.einsum("phqk,pkhd->pqhd", probs, value_heads, preferred_element_type=jnp.float32)
    return mixed.reshape(periods, row_count, features)


def silu_parts(pre):
    sigma = jax.nn.sigmoid(pre)
    return (pre * sigma, sigma * (1.0 + pre * (1.0 - sigma)))


def partial_grads(casted, key_norm, targets):
    gate_pre = jnp.einsum("thi,hji->htj", key_norm, casted[0], preferred_element_type=jnp.float32)
    up_pre = jnp.einsum("thi,hji->htj", key_norm, casted[1], preferred_element_type=jnp.float32)
    active, slope = silu_parts(gate_pre)
    hidden = (active * up_pre).astype(jnp.bfloat16)
    back = -jnp.einsum("tho,hoj->htj", targets, casted[2], preferred_element_type=jnp.float32)
    d_gate = (back * up_pre * slope).astype(jnp.bfloat16)
    d_up = (back * active).astype(jnp.bfloat16)
    g_gate = jnp.einsum("htj,thi->hji", d_gate, key_norm, preferred_element_type=jnp.float32)
    g_up = jnp.einsum("htj,thi->hji", d_up, key_norm, preferred_element_type=jnp.float32)
    g_down = -jnp.einsum("tho,htj->hoj", targets, hidden, preferred_element_type=jnp.float32)
    return jnp.stack([g_gate, g_up, g_down])


def apply_fast(casted, query_norm, fast_gain):
    gate_pre = jnp.einsum("thi,hji->htj", query_norm, casted[0], preferred_element_type=jnp.float32)
    up_pre = jnp.einsum("thi,hji->htj", query_norm, casted[1], preferred_element_type=jnp.float32)
    hidden = (jax.nn.silu(gate_pre) * up_pre).astype(jnp.bfloat16)
    result = jnp.einsum("htj,hoj->tho", hidden, casted[2], preferred_element_type=jnp.float32)
    return rms_rows(result) * fast_gain[None]


def advance(weights, moment, summed, rate_total):
    moment = MOMENT_DECAY * moment + summed / rate_total[None, :, None, None]
    weights = weights - STEP_RATE * rms_rows(moment)
    return (weights, moment)


def spread_rows(weights):
    return lax.all_gather(weights.astype(jnp.bfloat16), "seq", axis=2, tiled=True)


def split_shards(token_queries, token_keys, token_values, step_size, fast_weights, momentum, fast_gain):
    periods, row_count, features = token_queries.shape
    head_count = features // HD
    head_width = fast_weights.shape[3]
    fast_heads = features // head_width
    seq_place = lax.axis_index("seq")
    leading = seq_place == 0
    tail_rows = shifted((token_keys, token_values), "seq", 1)
    halo_keys = jnp.where(leading, jnp.roll(tail_rows[0], 1, axis=0), tail_rows[0])
    halo_values = jnp.where(leading, jnp.roll(tail_rows[1], 1, axis=0), tail_rows[1])
    halo_live = jnp.logical_or(jnp.logical_not(leading), jnp.arange(periods, dtype=jnp.int32) > 0)
    key_all = jnp.concatenate([halo_keys, token_keys], 1)
    value_all = jnp.concatenate([halo_values, token_values], 1)
    mixed_all = attend(token_queries, key_all, value_all, halo_live, head_count)
    weight_state, moment_state = (fast_weights, momentum)
    casted = spread_rows(weight_state)
    outputs = []
    for period in range(periods):
        rates = step_size[:, period]
        key_norm = rms_rows(
            token_keys[period].reshape(row_count, fast_heads, head_width).astype(jnp.float32)
        ).astype(jnp.bfloat16)
        targets = (
            rates.T[:, :, None]
            * token_values[period].reshape(row_count, fast_heads, head_width).astype(jnp.float32)
        ).astype(jnp.bfloat16)
        partial_value = partial_grads(casted, key_norm, targets)
        rate_total = lax.psum(jnp.sum(rates, axis=1), "seq")
        summed = lax.psum_scatter(
            partial_value.astype(jnp.bfloat16), "seq", scatter_dimension=2, tiled=True
        ).astype(jnp.float32)
        weight_state, moment_state = advance(weight_state, moment_state, summed, rate_total)
        casted = spread_rows(weight_state)
        query_norm = rms_rows(
            token_queries[period].reshape(row_count, fast_heads, head_width).astype(jnp.float32)
        ).astype(jnp.bfloat16)
        fast_out = apply_fast(casted, query_norm, fast_gain).reshape(row_count, features)
        outputs.append((mixed_all[period] + fast_out).astype(jnp.bfloat16))
    return (jnp.stack(outputs), weight_state, moment_state)


def dot_rows(x, y):
    return lax.dot_general(x, y, (((1,), (1,)), ((), ())), preferred_element_type=jnp.float32)


def dot_tokens(x, y):
    return lax.dot_general(x, y, (((0,), (0,)), ((), ())), preferred_element_type=jnp.float32)


def dot_plain(x, y):
    return lax.dot_general(x, y, (((1,), (0,)), ((), ())), preferred_element_type=jnp.float32)


def hub_kernel(
    n,
    periods,
    q_ref,
    k_ref,
    v_ref,
    r_ref,
    w_ref,
    m_ref,
    gain_ref,
    layer_ref,
    nw_ref,
    nm_ref,
    wb_ref,
    mb_ref,
    qb,
    kb,
    vb,
    rb,
    wblk,
    mblk,
    wf,
    mf,
    gacc,
    gs,
    gin,
    lbuf,
    fast,
    in_send,
    in_recv,
    g_send,
    g_recv,
    l_send,
    l_recv,
):
    half = n // 2
    me = lax.axis_index("seq")
    rows, width = kb.shape[1], kb.shape[2]
    share = width // n
    left = me < half
    near_h = jnp.where(left, 0, 1)
    far_h = 1 - near_h
    near_hub = half - 1 + near_h
    far_hub = half - 1 + far_h
    is_hub = me == near_hub
    mesh_id = pl.DeviceIdType.MESH

    barrier = pltpu.get_barrier_semaphore()
    for z in range(n):

        @pl.when(me != z)
        def _():
            pl.semaphore_signal(barrier, inc=1, device_id={"seq": z}, device_id_type=mesh_id)

    pl.semaphore_wait(barrier, n - 1)

    def columns(h):
        return pl.ds(pl.multiple_of(h * width, width), width)

    def own_rows(z):
        return pl.ds(pl.multiple_of(z * share, share), share)

    inward = []

    def tokens(ref, buf, p):
        return (lambda h: ref.at[p, :, columns(h)], lambda z: buf.at[p * n + z])

    kind = {}
    for p in range(periods):
        kind["k", p] = len(inward)
        inward.append(tokens(k_ref, kb, p))
        kind["v", p] = len(inward)
        inward.append(tokens(v_ref, vb, p))
        if p == 0:
            kind["w"] = len(inward)
            inward.append((lambda h: wb_ref.at[:, h], lambda z: wblk.at[:, own_rows(z)]))
            kind["r"] = len(inward)
            inward.append((lambda h: r_ref.at[h], lambda z: rb.at[z]))
            kind["m"] = len(inward)
            inward.append((lambda h: mb_ref.at[:, h], lambda z: mblk.at[:, own_rows(z)]))
        kind["q", p] = len(inward)
        inward.append(tokens(q_ref, qb, p))

    def in_remote(i, h, hub, which, z):
        src, dst = inward[i]
        return pltpu.make_async_remote_copy(
            src_ref=src(h),
            dst_ref=dst(z),
            send_sem=in_send.at[i, which],
            recv_sem=in_recv.at[i, z],
            device_id={"seq": hub},
            device_id_type=mesh_id,
        )

    def in_local(i):
        src, dst = inward[i]
        return pltpu.make_async_copy(src(near_h), dst(me), in_recv.at[i, me])

    for i in range(len(inward)):
        if i == kind["w"]:
            wb_ref[...] = w_ref[...].astype(jnp.bfloat16)
            mb_ref[...] = m_ref[...].astype(jnp.bfloat16)

        @pl.when(is_hub)
        def _():
            in_local(i).start()
            in_remote(i, far_h, far_hub, 1, me).start()

        @pl.when(jnp.logical_not(is_hub))
        def _():
            in_remote(i, near_h, near_hub, 0, me).start()

    @pl.when(jnp.logical_not(is_hub))
    def _():
        for i in range(len(inward)):
            in_remote(i, far_h, far_hub, 1, me).start()

    def await_in(i):
        for z in range(n):

            @pl.when(me == z)
            def _():
                in_local(i).wait()

            @pl.when(me != z)
            def _():
                in_remote(i, near_h, far_hub, 0, z).wait_recv()

    def out_remote(what, p, z, h):
        if what == "g":
            src, dst, ss, rs = gs.at[p, z], gin.at[p, h], g_send, g_recv
        else:
            src, dst = lbuf.at[p * n + z], layer_ref.at[p, :, columns(h)]
            ss, rs = l_send, l_recv
        return pltpu.make_async_remote_copy(
            src_ref=src,
            dst_ref=dst,
            send_sem=ss.at[p, z],
            recv_sem=rs.at[p, h],
            device_id={"seq": z},
            device_id_type=mesh_id,
        )

    def out_local(what, p):
        if what == "g":
            return pltpu.make_async_copy(gs.at[p, me], gin.at[p, near_h], g_recv.at[p, near_h])
        return pltpu.make_async_copy(
            lbuf.at[p * n + me], layer_ref.at[p, :, columns(near_h)], l_recv.at[p, near_h]
        )

    def send_near(what, p):
        out_local(what, p).start()
        for z in range(n):
            same_side = left if z < half else jnp.logical_not(left)

            @pl.when(jnp.logical_and(same_side, me != z))
            def _():
                out_remote(what, p, z, near_h).start()

    def send_far(what, p):
        for z in [*range(half), *reversed(range(half, n))]:
            other_side = jnp.logical_not(left) if z < half else left

            @pl.when(other_side)
            def _():
                out_remote(what, p, z, near_h).start()

    def await_out(what, p):
        for h in range(2):

            @pl.when(me == half - 1 + h)
            def _():
                out_local(what, p).wait()

            @pl.when(me != half - 1 + h)
            def _():
                out_remote(what, p, half - 1 + h, h).wait_recv()

    def rate_total(p):
        total = jnp.sum(rb[0, p : p + 1, :], axis=1, keepdims=True)
        for z in range(1, n):
            total = total + jnp.sum(rb[z, p : p + 1, :], axis=1, keepdims=True)
        return total

    @pl.when(is_hub)
    def _():
        gain = gain_ref[pl.ds(near_h, 1), :]
        row_pos = lax.broadcasted_iota(jnp.int32, (rows, rows), 0)
        col_pos = lax.broadcasted_iota(jnp.int32, (rows, rows), 1)
        causal = col_pos <= row_pos
        await_in(kind["w"])
        await_in(kind["r"])
        for p in range(periods):
            await_in(kind["k", p])
            await_in(kind["v", p])
            if p > 0:
                send_far("g", p - 1)
                send_far("l", p - 1)
            gacc[...] = jnp.zeros_like(gacc)

            def grad_step(z, carry):
                key_norm = rms_rows(kb[p * n + z].astype(jnp.float32)).astype(jnp.bfloat16)
                gate_pre = dot_rows(key_norm, wblk[0])
                up_pre = dot_rows(key_norm, wblk[1])
                rates = jnp.broadcast_to(rb[z, p : p + 1, :], (HD, rows)).T[:, :1]
                targets = (rates * vb[p * n + z].astype(jnp.float32)).astype(jnp.bfloat16)
                back = -dot_plain(targets, wblk[2])
                active, slope = silu_parts(gate_pre)
                hidden = (active * up_pre).astype(jnp.bfloat16)
                d_gate = (back * up_pre * slope).astype(jnp.bfloat16)
                d_up = (back * active).astype(jnp.bfloat16)
                gacc[0] += dot_tokens(d_gate, key_norm)
                gacc[1] += dot_tokens(d_up, key_norm)
                gacc[2] -= dot_tokens(targets, hidden)
                return carry

            lax.fori_loop(0, n, grad_step, 0)
            if p == 0:
                await_in(kind["m"])
            total = rate_total(p)

            def update_step(z, carry):
                part = own_rows(z)
                for i in range(3):
                    step = gacc[i, part, :] / total
                    gs[p, z, i] = step.astype(jnp.bfloat16)
                    old_m = mblk[i, part, :].astype(jnp.float32) if p == 0 else mf[i, part, :]
                    old_w = wblk[i, part, :].astype(jnp.float32) if p == 0 else wf[i, part, :]
                    moment = MOMENT_DECAY * old_m + step
                    weight = old_w - STEP_RATE * rms_rows(moment)
                    mf[i, part, :] = moment
                    wf[i, part, :] = weight
                    wblk[i, part, :] = weight.astype(jnp.bfloat16)
                return carry

            lax.fori_loop(0, n, update_step, 0)
            if p == periods - 1:
                send_far("g", p)
            send_near("g", p)
            await_in(kind["q", p])

            def apply_step(z, carry):
                g = p * n + z
                query_norm = rms_rows(qb[g].astype(jnp.float32)).astype(jnp.bfloat16)
                gate_pre = dot_rows(query_norm, wblk[0])
                up_pre = dot_rows(query_norm, wblk[1])
                hidden = (jax.nn.silu(gate_pre) * up_pre).astype(jnp.bfloat16)
                fast[...] = rms_rows(dot_rows(hidden, wblk[2])) * gain
                before = jnp.maximum(g - 1, 0)
                for head in range(width // HD):
                    cut = slice(head * HD, (head + 1) * HD)
                    query = qb[g, :, cut]
                    here = dot_rows(query, kb[g, :, cut])
                    past = dot_rows(query, kb[before, :, cut])
                    past = jnp.where(g > 0, past, -1e30 * math.sqrt(HD))
                    scores = jnp.where(causal, here, past) * (1.0 / math.sqrt(HD))
                    top = jnp.max(scores, axis=-1, keepdims=True)
                    expo = jnp.exp(scores - top)
                    probs = expo / jnp.sum(expo, axis=-1, keepdims=True)
                    own = jnp.where(causal, probs, 0.0).astype(jnp.bfloat16)
                    old = jnp.where(causal, 0.0, probs).astype(jnp.bfloat16)
                    mixed = dot_plain(own, vb[g, :, cut]) + dot_plain(old, vb[before, :, cut])
                    lbuf[g, :, cut] = (mixed + fast[:, cut]).astype(jnp.bfloat16)
                return carry

            lax.fori_loop(0, n, apply_step, 0)
            if p == periods - 1:
                send_far("l", p)
            send_near("l", p)

    def own_step(h):
        for i in range(3):
            moment = m_ref[i, h]
            weight = w_ref[i, h]
            for p in range(periods):
                moment = MOMENT_DECAY * moment + gin[p, h, i].astype(jnp.float32)
                weight = weight - STEP_RATE * rms_rows(moment)
            nm_ref[i, h] = moment
            nw_ref[i, h] = weight

    for p in range(periods):
        await_out("g", p)
    for h in range(2):
        own_step(h)
    for p in range(periods):
        await_out("l", p)

    @pl.when(is_hub)
    def _():
        for p in range(periods):
            for z in range(n):

                @pl.when(me != z)
                def _():
                    out_remote("g", p, z, near_h).wait_send()
                    out_remote("l", p, z, near_h).wait_send()

    for i in range(len(inward)):
        in_remote(i, far_h, far_hub, 1, me).wait_send()

        @pl.when(jnp.logical_not(is_hub))
        def _():
            in_remote(i, near_h, near_hub, 0, me).wait_send()


def hub_shards(
    token_queries, token_keys, token_values, step_size, fast_weights, momentum, fast_gain
):
    periods, rows, features = token_queries.shape
    parts, heads, share, width = fast_weights.shape
    n = lax.axis_size("seq")
    bf16, f32 = jnp.bfloat16, jnp.float32
    kinds = 3 + 3 * periods
    vmem = pl.BlockSpec(memory_space=pltpu.VMEM)
    anywhere = pl.BlockSpec(memory_space=pl.ANY)
    square = (parts, width, width)
    stream = pltpu.VMEM((periods * n, rows, width), bf16)
    dma = pltpu.SemaphoreType.DMA
    return pl.pallas_call(
        functools.partial(hub_kernel, n, periods),
        out_shape=(
            jax.ShapeDtypeStruct(token_queries.shape, bf16),
            jax.ShapeDtypeStruct(fast_weights.shape, f32),
            jax.ShapeDtypeStruct(momentum.shape, f32),
        ),
        in_specs=[anywhere] * 4 + [vmem] * 3,
        out_specs=(vmem, vmem, vmem),
        scratch_shapes=[
            pltpu.VMEM(fast_weights.shape, bf16),
            pltpu.VMEM(momentum.shape, bf16),
            stream,
            stream,
            stream,
            pltpu.VMEM((n, periods, rows), f32),
            pltpu.VMEM(square, bf16),
            pltpu.VMEM(square, bf16),
            pltpu.VMEM(square, f32),
            pltpu.VMEM(square, f32),
            pltpu.VMEM(square, f32),
            pltpu.VMEM((periods, n, parts, share, width), bf16),
            pltpu.VMEM((periods, heads, parts, share, width), bf16),
            stream,
            pltpu.VMEM((rows, width), f32),
            dma((kinds, 2)),
            dma((kinds, n)),
            dma((periods, n)),
            dma((periods, heads)),
            dma((periods, n)),
            dma((periods, heads)),
        ],
        compiler_params=pltpu.CompilerParams(
            collective_id=0, has_side_effects=True, vmem_limit_bytes=56 * 1024 * 1024
        ),
    )(
        token_queries,
        token_keys,
        token_values,
        step_size,
        fast_weights,
        momentum,
        fast_gain,
    )


def shards(token_queries, token_keys, token_values, step_size, fast_weights, momentum, fast_gain):
    args = (
        token_queries,
        token_keys,
        token_values,
        step_size,
        fast_weights,
        momentum,
        fast_gain,
    )
    n = lax.axis_size("seq")
    two_hubs = fast_weights.shape[1] == 2 and n % 2 == 0 and token_queries.shape[1] == WINDOW
    return hub_shards(*args) if two_hubs else split_shards(*args)


def solution(mesh):
    placed = (
        P("grp", "seq", "head"),
        P("grp", "seq", "head"),
        P("grp", "seq", "head"),
        P("head", "grp", "seq"),
        P("grp", "head", "seq", None),
        P("grp", "head", "seq", None),
        P("head", None),
    )
    return jax.shard_map(
        shards,
        mesh=mesh,
        in_specs=placed,
        out_specs=(
            P("grp", "seq", "head"),
            P("grp", "head", "seq", None),
            P("grp", "head", "seq", None),
        ),
        check_vma=False,
    )
```

```python
import functools
import math

import jax
import jax.numpy as jnp
from jax import lax
from jax.experimental import pallas as pl
from jax.experimental.pallas import tpu as pltpu
from jax.sharding import PartitionSpec as P

HD = 128
WINDOW = 256


EPSILON = 1e-06
MOMENT_DECAY = 0.9
STEP_RATE = 0.02


def shifted(block, axis, distance):
    devices = range(lax.axis_size(axis))
    route = [((i - distance) % len(devices), i) for i in devices]
    return lax.ppermute(block, axis, route)


def rms_rows(values):
    return values * lax.rsqrt(jnp.mean(values * values, axis=-1, keepdims=True) + EPSILON)


def attend(query_rows, key_rows, value_rows, halo_live, head_count):
    periods, row_count, features = query_rows.shape
    key_span = key_rows.shape[1]
    query_heads = query_rows.reshape(periods, row_count, head_count, HD)
    key_heads = key_rows.reshape(periods, key_span, head_count, HD)
    value_heads = value_rows.reshape(periods, key_span, head_count, HD)
    scores = jnp.einsum(
        "pqhd,pkhd->phqk", query_heads, key_heads, preferred_element_type=jnp.float32
    )
    scores = scores * (1.0 / math.sqrt(HD))
    query_pos = lax.broadcasted_iota(jnp.int32, (row_count, key_span), 0)
    key_pos = lax.broadcasted_iota(jnp.int32, (row_count, key_span), 1) - (key_span - row_count)
    band = (key_pos <= query_pos) & (key_pos > query_pos - WINDOW)
    allowed = band[None] & ((key_pos >= 0)[None] | halo_live[:, None, None])
    scores = jnp.where(allowed[:, None], scores, -1e30)
    top = jnp.max(scores, axis=-1, keepdims=True)
    expo = jnp.exp(scores - top)
    probs = (expo / jnp.sum(expo, axis=-1, keepdims=True)).astype(jnp.bfloat16)
    mixed = jnp.einsum("phqk,pkhd->pqhd", probs, value_heads, preferred_element_type=jnp.float32)
    return mixed.reshape(periods, row_count, features)


def silu_parts(pre):
    sigma = jax.nn.sigmoid(pre)
    return (pre * sigma, sigma * (1.0 + pre * (1.0 - sigma)))


def partial_grads(casted, key_norm, targets):
    gate_pre = jnp.einsum("thi,hji->htj", key_norm, casted[0], preferred_element_type=jnp.float32)
    up_pre = jnp.einsum("thi,hji->htj", key_norm, casted[1], preferred_element_type=jnp.float32)
    active, slope = silu_parts(gate_pre)
    hidden = (active * up_pre).astype(jnp.bfloat16)
    back = -jnp.einsum("tho,hoj->htj", targets, casted[2], preferred_element_type=jnp.float32)
    d_gate = (back * up_pre * slope).astype(jnp.bfloat16)
    d_up = (back * active).astype(jnp.bfloat16)
    g_gate = jnp.einsum("htj,thi->hji", d_gate, key_norm, preferred_element_type=jnp.float32)
    g_up = jnp.einsum("htj,thi->hji", d_up, key_norm, preferred_element_type=jnp.float32)
    g_down = -jnp.einsum("tho,htj->hoj", targets, hidden, preferred_element_type=jnp.float32)
    return jnp.stack([g_gate, g_up, g_down])


def apply_fast(casted, query_norm, fast_gain):
    gate_pre = jnp.einsum("thi,hji->htj", query_norm, casted[0], preferred_element_type=jnp.float32)
    up_pre = jnp.einsum("thi,hji->htj", query_norm, casted[1], preferred_element_type=jnp.float32)
    hidden = (jax.nn.silu(gate_pre) * up_pre).astype(jnp.bfloat16)
    result = jnp.einsum("htj,hoj->tho", hidden, casted[2], preferred_element_type=jnp.float32)
    return rms_rows(result) * fast_gain[None]


def advance(weights, moment, summed, rate_total):
    moment = MOMENT_DECAY * moment + summed / rate_total[None, :, None, None]
    weights = weights - STEP_RATE * rms_rows(moment)
    return (weights, moment)


def spread_rows(weights):
    return lax.all_gather(weights.astype(jnp.bfloat16), "seq", axis=2, tiled=True)


def split_shards(token_queries, token_keys, token_values, step_size, fast_weights, momentum, fast_gain):
    periods, row_count, features = token_queries.shape
    head_count = features // HD
    head_width = fast_weights.shape[3]
    fast_heads = features // head_width
    seq_place = lax.axis_index("seq")
    leading = seq_place == 0
    tail_rows = shifted((token_keys, token_values), "seq", 1)
    halo_keys = jnp.where(leading, jnp.roll(tail_rows[0], 1, axis=0), tail_rows[0])
    halo_values = jnp.where(leading, jnp.roll(tail_rows[1], 1, axis=0), tail_rows[1])
    halo_live = jnp.logical_or(jnp.logical_not(leading), jnp.arange(periods, dtype=jnp.int32) > 0)
    key_all = jnp.concatenate([halo_keys, token_keys], 1)
    value_all = jnp.concatenate([halo_values, token_values], 1)
    mixed_all = attend(token_queries, key_all, value_all, halo_live, head_count)
    weight_state, moment_state = (fast_weights, momentum)
    casted = spread_rows(weight_state)
    outputs = []
    for period in range(periods):
        rates = step_size[:, period]
        key_norm = rms_rows(
            token_keys[period].reshape(row_count, fast_heads, head_width).astype(jnp.float32)
        ).astype(jnp.bfloat16)
        targets = (
            rates.T[:, :, None]
            * token_values[period].reshape(row_count, fast_heads, head_width).astype(jnp.float32)
        ).astype(jnp.bfloat16)
        partial_value = partial_grads(casted, key_norm, targets)
        rate_total = lax.psum(jnp.sum(rates, axis=1), "seq")
        summed = lax.psum_scatter(
            partial_value.astype(jnp.bfloat16), "seq", scatter_dimension=2, tiled=True
        ).astype(jnp.float32)
        weight_state, moment_state = advance(weight_state, moment_state, summed, rate_total)
        casted = spread_rows(weight_state)
        query_norm = rms_rows(
            token_queries[period].reshape(row_count, fast_heads, head_width).astype(jnp.float32)
        ).astype(jnp.bfloat16)
        fast_out = apply_fast(casted, query_norm, fast_gain).reshape(row_count, features)
        outputs.append((mixed_all[period] + fast_out).astype(jnp.bfloat16))
    return (jnp.stack(outputs), weight_state, moment_state)


def dot_rows(x, y):
    return lax.dot_general(x, y, (((1,), (1,)), ((), ())), preferred_element_type=jnp.float32)


def dot_tokens(x, y):
    return lax.dot_general(x, y, (((0,), (0,)), ((), ())), preferred_element_type=jnp.float32)


def dot_plain(x, y):
    return lax.dot_general(x, y, (((1,), (0,)), ((), ())), preferred_element_type=jnp.float32)


def hub_kernel(
    n,
    periods,
    q_ref,
    k_ref,
    v_ref,
    r_ref,
    w_ref,
    m_ref,
    gain_ref,
    layer_ref,
    nw_ref,
    nm_ref,
    wb_ref,
    mb_ref,
    qb,
    kb,
    vb,
    rb,
    wblk,
    mblk,
    wf,
    mf,
    gacc,
    gs,
    gin,
    lbuf,
    fast,
    in_send,
    in_recv,
    g_send,
    g_recv,
    l_send,
    l_recv,
):
    half = n // 2
    me = lax.axis_index("seq")
    rows, width = kb.shape[1], kb.shape[2]
    share = width // n
    left = me < half
    near_h = jnp.where(left, 0, 1)
    far_h = 1 - near_h
    near_hub = half - 1 + near_h
    far_hub = half - 1 + far_h
    is_hub = me == near_hub
    mesh_id = pl.DeviceIdType.MESH

    barrier = pltpu.get_barrier_semaphore()
    for z in range(n):

        @pl.when(me != z)
        def _():
            pl.semaphore_signal(barrier, inc=1, device_id={"seq": z}, device_id_type=mesh_id)

    pl.semaphore_wait(barrier, n - 1)

    def columns(h):
        return pl.ds(pl.multiple_of(h * width, width), width)

    def own_rows(z):
        return pl.ds(pl.multiple_of(z * share, share), share)

    inward = []

    def tokens(ref, buf, p):
        return (lambda h: ref.at[p, :, columns(h)], lambda z: buf.at[p * n + z])

    kind = {}
    for p in range(periods):
        kind["k", p] = len(inward)
        inward.append(tokens(k_ref, kb, p))
        kind["v", p] = len(inward)
        inward.append(tokens(v_ref, vb, p))
        if p == 0:
            kind["w"] = len(inward)
            inward.append((lambda h: wb_ref.at[:, h], lambda z: wblk.at[:, own_rows(z)]))
            kind["r"] = len(inward)
            inward.append((lambda h: r_ref.at[h], lambda z: rb.at[z]))
            kind["m"] = len(inward)
            inward.append((lambda h: mb_ref.at[:, h], lambda z: mblk.at[:, own_rows(z)]))
        kind["q", p] = len(inward)
        inward.append(tokens(q_ref, qb, p))

    def in_remote(i, h, hub, which, z):
        src, dst = inward[i]
        return pltpu.make_async_remote_copy(
            src_ref=src(h),
            dst_ref=dst(z),
            send_sem=in_send.at[i, which],
            recv_sem=in_recv.at[i, z],
            device_id={"seq": hub},
            device_id_type=mesh_id,
        )

    def in_local(i):
        src, dst = inward[i]
        return pltpu.make_async_copy(src(near_h), dst(me), in_recv.at[i, me])

    for i in range(len(inward)):
        if i == kind["w"]:
            wb_ref[...] = w_ref[...].astype(jnp.bfloat16)
            mb_ref[...] = m_ref[...].astype(jnp.bfloat16)
        in_remote(i, far_h, far_hub, 1, me).start()

        @pl.when(is_hub)
        def _():
            in_local(i).start()

        @pl.when(jnp.logical_not(is_hub))
        def _():
            in_remote(i, near_h, near_hub, 0, me).start()

    def await_in(i):
        for z in range(n):

            @pl.when(me == z)
            def _():
                in_local(i).wait()

            @pl.when(me != z)
            def _():
                in_remote(i, near_h, far_hub, 0, z).wait_recv()

    def out_remote(what, p, z, h):
        if what == "g":
            src, dst, ss, rs = gs.at[p, z], gin.at[p, h], g_send, g_recv
        else:
            src, dst = lbuf.at[p * n + z], layer_ref.at[p, :, columns(h)]
            ss, rs = l_send, l_recv
        return pltpu.make_async_remote_copy(
            src_ref=src,
            dst_ref=dst,
            send_sem=ss.at[p, z],
            recv_sem=rs.at[p, h],
            device_id={"seq": z},
            device_id_type=mesh_id,
        )

    def out_local(what, p):
        if what == "g":
            return pltpu.make_async_copy(gs.at[p, me], gin.at[p, near_h], g_recv.at[p, near_h])
        return pltpu.make_async_copy(
            lbuf.at[p * n + me], layer_ref.at[p, :, columns(near_h)], l_recv.at[p, near_h]
        )

    def send_near(what, p):
        out_local(what, p).start()
        for z in range(n):
            same_side = left if z < half else jnp.logical_not(left)

            @pl.when(jnp.logical_and(same_side, me != z))
            def _():
                out_remote(what, p, z, near_h).start()

    def send_far(what, p):
        for z in [*range(half), *reversed(range(half, n))]:
            other_side = jnp.logical_not(left) if z < half else left

            @pl.when(other_side)
            def _():
                out_remote(what, p, z, near_h).start()

    def await_out(what, p):
        for h in range(2):

            @pl.when(me == half - 1 + h)
            def _():
                out_local(what, p).wait()

            @pl.when(me != half - 1 + h)
            def _():
                out_remote(what, p, half - 1 + h, h).wait_recv()

    def rate_total(p):
        total = jnp.sum(rb[0, p : p + 1, :], axis=1, keepdims=True)
        for z in range(1, n):
            total = total + jnp.sum(rb[z, p : p + 1, :], axis=1, keepdims=True)
        return total

    @pl.when(is_hub)
    def _():
        gain = gain_ref[pl.ds(near_h, 1), :]
        row_pos = lax.broadcasted_iota(jnp.int32, (rows, rows), 0)
        col_pos = lax.broadcasted_iota(jnp.int32, (rows, rows), 1)
        causal = col_pos <= row_pos
        await_in(kind["w"])
        await_in(kind["r"])
        for p in range(periods):
            await_in(kind["k", p])
            await_in(kind["v", p])
            if p > 0:
                send_far("g", p - 1)
                send_far("l", p - 1)
            gacc[...] = jnp.zeros_like(gacc)

            def grad_step(z, carry):
                key_norm = rms_rows(kb[p * n + z].astype(jnp.float32)).astype(jnp.bfloat16)
                gate_pre = dot_rows(key_norm, wblk[0])
                up_pre = dot_rows(key_norm, wblk[1])
                rates = jnp.broadcast_to(rb[z, p : p + 1, :], (HD, rows)).T[:, :1]
                targets = (rates * vb[p * n + z].astype(jnp.float32)).astype(jnp.bfloat16)
                back = -dot_plain(targets, wblk[2])
                active, slope = silu_parts(gate_pre)
                hidden = (active * up_pre).astype(jnp.bfloat16)
                d_gate = (back * up_pre * slope).astype(jnp.bfloat16)
                d_up = (back * active).astype(jnp.bfloat16)
                gacc[0] += dot_tokens(d_gate, key_norm)
                gacc[1] += dot_tokens(d_up, key_norm)
                gacc[2] -= dot_tokens(targets, hidden)
                return carry

            lax.fori_loop(0, n, grad_step, 0)
            if p == 0:
                await_in(kind["m"])
            total = rate_total(p)

            def update_step(z, carry):
                part = own_rows(z)
                for i in range(3):
                    step = gacc[i, part, :] / total
                    gs[p, z, i] = step.astype(jnp.bfloat16)
                    old_m = mblk[i, part, :].astype(jnp.float32) if p == 0 else mf[i, part, :]
                    old_w = wblk[i, part, :].astype(jnp.float32) if p == 0 else wf[i, part, :]
                    moment = MOMENT_DECAY * old_m + step
                    weight = old_w - STEP_RATE * rms_rows(moment)
                    mf[i, part, :] = moment
                    wf[i, part, :] = weight
                    wblk[i, part, :] = weight.astype(jnp.bfloat16)
                return carry

            lax.fori_loop(0, n, update_step, 0)
            if p == periods - 1:
                send_far("g", p)
            send_near("g", p)
            await_in(kind["q", p])

            def apply_step(z, carry):
                g = p * n + z
                query_norm = rms_rows(qb[g].astype(jnp.float32)).astype(jnp.bfloat16)
                gate_pre = dot_rows(query_norm, wblk[0])
                up_pre = dot_rows(query_norm, wblk[1])
                hidden = (jax.nn.silu(gate_pre) * up_pre).astype(jnp.bfloat16)
                fast[...] = rms_rows(dot_rows(hidden, wblk[2])) * gain
                before = jnp.maximum(g - 1, 0)
                for head in range(width // HD):
                    cut = slice(head * HD, (head + 1) * HD)
                    query = qb[g, :, cut]
                    here = dot_rows(query, kb[g, :, cut])
                    past = dot_rows(query, kb[before, :, cut])
                    past = jnp.where(g > 0, past, -1e30 * math.sqrt(HD))
                    scores = jnp.where(causal, here, past) * (1.0 / math.sqrt(HD))
                    top = jnp.max(scores, axis=-1, keepdims=True)
                    expo = jnp.exp(scores - top)
                    probs = expo / jnp.sum(expo, axis=-1, keepdims=True)
                    own = jnp.where(causal, probs, 0.0).astype(jnp.bfloat16)
                    old = jnp.where(causal, 0.0, probs).astype(jnp.bfloat16)
                    mixed = dot_plain(own, vb[g, :, cut]) + dot_plain(old, vb[before, :, cut])
                    lbuf[g, :, cut] = (mixed + fast[:, cut]).astype(jnp.bfloat16)
                return carry

            lax.fori_loop(0, n, apply_step, 0)
            if p == periods - 1:
                send_far("l", p)
            send_near("l", p)

    def own_step(h):
        for i in range(3):
            moment = m_ref[i, h]
            weight = w_ref[i, h]
            for p in range(periods):
                moment = MOMENT_DECAY * moment + gin[p, h, i].astype(jnp.float32)
                weight = weight - STEP_RATE * rms_rows(moment)
            nm_ref[i, h] = moment
            nw_ref[i, h] = weight

    for p in range(periods):
        await_out("g", p)
    for h in range(2):
        own_step(h)
    for p in range(periods):
        await_out("l", p)

    @pl.when(is_hub)
    def _():
        for p in range(periods):
            for z in range(n):

                @pl.when(me != z)
                def _():
                    out_remote("g", p, z, near_h).wait_send()
                    out_remote("l", p, z, near_h).wait_send()

    for i in range(len(inward)):
        in_remote(i, far_h, far_hub, 1, me).wait_send()

        @pl.when(jnp.logical_not(is_hub))
        def _():
            in_remote(i, near_h, near_hub, 0, me).wait_send()


def hub_shards(
    token_queries, token_keys, token_values, step_size, fast_weights, momentum, fast_gain
):
    periods, rows, features = token_queries.shape
    parts, heads, share, width = fast_weights.shape
    n = lax.axis_size("seq")
    bf16, f32 = jnp.bfloat16, jnp.float32
    kinds = 3 + 3 * periods
    vmem = pl.BlockSpec(memory_space=pltpu.VMEM)
    anywhere = pl.BlockSpec(memory_space=pl.ANY)
    square = (parts, width, width)
    stream = pltpu.VMEM((periods * n, rows, width), bf16)
    dma = pltpu.SemaphoreType.DMA
    return pl.pallas_call(
        functools.partial(hub_kernel, n, periods),
        out_shape=(
            jax.ShapeDtypeStruct(token_queries.shape, bf16),
            jax.ShapeDtypeStruct(fast_weights.shape, f32),
            jax.ShapeDtypeStruct(momentum.shape, f32),
        ),
        in_specs=[anywhere] * 4 + [vmem] * 3,
        out_specs=(vmem, vmem, vmem),
        scratch_shapes=[
            pltpu.VMEM(fast_weights.shape, bf16),
            pltpu.VMEM(momentum.shape, bf16),
            stream,
            stream,
            stream,
            pltpu.VMEM((n, periods, rows), f32),
            pltpu.VMEM(square, bf16),
            pltpu.VMEM(square, bf16),
            pltpu.VMEM(square, f32),
            pltpu.VMEM(square, f32),
            pltpu.VMEM(square, f32),
            pltpu.VMEM((periods, n, parts, share, width), bf16),
            pltpu.VMEM((periods, heads, parts, share, width), bf16),
            stream,
            pltpu.VMEM((rows, width), f32),
            dma((kinds, 2)),
            dma((kinds, n)),
            dma((periods, n)),
            dma((periods, heads)),
            dma((periods, n)),
            dma((periods, heads)),
        ],
        compiler_params=pltpu.CompilerParams(
            collective_id=0, has_side_effects=True, vmem_limit_bytes=56 * 1024 * 1024
        ),
    )(
        token_queries,
        token_keys,
        token_values,
        step_size,
        fast_weights,
        momentum,
        fast_gain,
    )


def shards(token_queries, token_keys, token_values, step_size, fast_weights, momentum, fast_gain):
    args = (
        token_queries,
        token_keys,
        token_values,
        step_size,
        fast_weights,
        momentum,
        fast_gain,
    )
    n = lax.axis_size("seq")
    two_hubs = fast_weights.shape[1] == 2 and n % 2 == 0 and token_queries.shape[1] == WINDOW
    return hub_shards(*args) if two_hubs else split_shards(*args)


def solution(mesh):
    placed = (
        P("grp", "seq", "head"),
        P("grp", "seq", "head"),
        P("grp", "seq", "head"),
        P("head", "grp", "seq"),
        P("grp", "head", "seq", None),
        P("grp", "head", "seq", None),
        P("head", None),
    )
    return jax.shard_map(
        shards,
        mesh=mesh,
        in_specs=placed,
        out_specs=(
            P("grp", "seq", "head"),
            P("grp", "head", "seq", None),
            P("grp", "head", "seq", None),
        ),
        check_vma=False,
    )
```
